512 devices in a mesh: ctx: 128 (over z, x, core), tp: 4 (over y).
Axes of the slice: x: 4, y: 4, z: 16, core: 2. Of those that a mesh axis runs over, the one named last changes fastest.
Arguments:
- projected: bfloat16 [16384, 3, 4096], P('ctx', None, 'tp'), may hold values from -6 to 6
- short_taps: float32 [3, 7, 4096], P(None, None, 'tp'), may hold values from -2 to 2
- residues: float32 [4096, 16], P('tp'), may hold values from -6 to 6
- rates: float32 [4096, 16], P('tp'), may hold values from 0.3 to 1024
- skip_gain: float32 [4096], P('tp'), may hold values from -1 to 1
- norm_gain: float32 [4096], P('tp'), may hold values from 0.5 to 1.5
Outputs:
- mixed_out: bfloat16 [16384, 4096], P('ctx', 'tp')
The draws below stay inside these ranges and needn't reach their ends.
All inputs are finite; a program needn't handle non-finite values.
Results may differ from the reference program's by a relative error of at most 0.008.
Values may be sent and summed in bfloat16 or wider, within the bound.
No kernel may reach another device: no remote copies, remote signals or barrier semaphores. Data moves between devices by JAX's collectives and lax.ppermute only.
A program may use at most 64 MiB of HBM per device.

```python
import math
import jax
import jax.numpy as jnp
from jax import lax

D = 4096
MODES = 16
TAPS = 7
LENGTH = 16384


def draw_short_taps(key, part):
    base = jax.random.uniform(key, (3, TAPS, D), jnp.float32, -0.5, 0.5)
    chan = jnp.arange(D, dtype=jnp.int32).astype(jnp.float32) / D
    scale = jnp.power(3.0, 0.75 * chan)
    first = jnp.arange(3, dtype=jnp.int32)[:, None, None] == 0
    return jnp.where(first, base * scale[None, None, :], base)


def block_levels(rng, dims, cuts, smallest, largest):
    def one(dim, blocks):
        heights = jax.random.uniform(jax.random.fold_in(jax.random.fold_in(rng, 6), dim), (blocks,), jnp.float32, smallest / len(cuts), largest / len(cuts))
        return jnp.repeat(jnp.exp(heights), dims[dim] // blocks).reshape((-1,) + (1,) * (len(dims) - dim - 1))

    loudness = one(*cuts[0])
    for cut in cuts[1:]:
        loudness = loudness * one(*cut)
    return loudness


def centred(stream_key, shape, scale, bound, shards=(), held_as=jnp.bfloat16):
    factor_of = block_levels(stream_key, shape, shards, -0.22, 0.18) if shards else 1.0
    drawn = jax.random.normal(stream_key, shape, jnp.float32) * scale * factor_of
    return jnp.minimum(jnp.maximum(drawn, -bound), bound).astype(held_as)


def setup_inputs(seed: int = 0) -> dict:
    key_list = jax.random.split(jax.random.key(seed), 7)
    return {
        "projected": centred(key_list[0], (LENGTH, 3, D), 1.0, 6.0, ((0, 128), (2, 4))),
        "short_taps": draw_short_taps(jax.random.fold_in(key_list[6], 71), 0),
        "residues": centred(key_list[2], (D, MODES), 1.0, 6.0, ((0, 4),), jnp.float32),
        "rates": jnp.clip(jnp.exp(math.log(1024.0) - 8.135445 * jax.random.uniform(key_list[3], (D, MODES), jnp.float32) ** block_levels(key_list[3], (D, MODES), ((0, 4),), -0.2, 0.2)), 0.3, 1024.0),
        "skip_gain": jnp.clip(jax.random.uniform(key_list[4], (D,), jnp.float32, -1.0, 1.0) * block_levels(key_list[4], (D,), ((0, 4),), -0.4, 0.0), -1.0, 1.0),
        "norm_gain": jnp.clip(1.0 + 0.1 * jax.random.normal(key_list[5], (D,), jnp.float32), 0.5, 1.5),
    }


def reference(projected, short_taps, residues, rates, skip_gain, norm_gain):
    block = min(D, 256)
    count = D // block
    positions = jnp.arange(LENGTH, dtype=jnp.int32).astype(jnp.float32)

    def one_block(index):
        first = (index * block).astype(jnp.int32)
        piece = lax.dynamic_slice_in_dim(projected, first, block, 2).astype(jnp.float32)
        taps = lax.dynamic_slice_in_dim(short_taps, first, block, 2)
        res_block = lax.dynamic_slice_in_dim(residues, first, block, 0)
        rate_block = lax.dynamic_slice_in_dim(rates, first, block, 0)
        skip_block = lax.dynamic_slice_in_dim(skip_gain, first, block, 0)
        padded = jnp.pad(piece, ((TAPS - 1, 0), (0, 0), (0, 0)))
        mixed = jnp.zeros_like(piece)
        for offset in range(TAPS):
            mixed = mixed + taps[None, :, offset, :] * padded[TAPS - 1 - offset:TAPS - 1 - offset + LENGTH]
        query = mixed[:, 0]
        keyed = mixed[:, 1]
        valued = mixed[:, 2]
        product = (keyed * valued).astype(jnp.bfloat16)
        product_wide = lax.optimization_barrier(product).astype(jnp.float32)
        kernel = jnp.zeros((LENGTH, block), jnp.float32)
        for mode in range(MODES):
            kernel = kernel + res_block[:, mode][None, :] * jnp.exp(-(positions[:, None] * rate_block[:, mode][None, :]) / LENGTH)
        kernel = kernel / math.sqrt(LENGTH)
        spectrum = jnp.fft.rfft(product_wide, n=2 * LENGTH, axis=0) * jnp.fft.rfft(kernel, n=2 * LENGTH, axis=0)
        convolved = jnp.fft.irfft(spectrum, n=2 * LENGTH, axis=0)[:LENGTH]
        long_part = convolved.astype(jnp.bfloat16)
        long_wide = lax.optimization_barrier(long_part).astype(jnp.float32)
        return query * (long_wide + skip_block[None, :] * product_wide)
    blocks = lax.map(one_block, jnp.arange(count, dtype=jnp.int32))
    gated = jnp.transpose(blocks, (1, 0, 2)).reshape(LENGTH, D)
    mean_square = lax.optimization_barrier(jnp.sum(gated * gated, axis=1, keepdims=True)) / D
    return (gated * norm_gain[None, :] / jnp.sqrt(mean_square + 1e-05)).astype(jnp.bfloat16)
```

```python
import math

import jax
import jax.numpy as jnp
from jax import lax
from jax.experimental import pallas as pl
from jax.experimental.pallas import tpu as pltpu
from jax.sharding import PartitionSpec as P

TAPS = 7
MODES = 16
LANES = 128
SUB = 8
PLANE = 8
RIM = 8
HIGHEST = lax.Precision.HIGHEST
F32 = jnp.float32


def whole(memory_space=pltpu.VMEM):
    return pl.BlockSpec(memory_space=memory_space)


def spread(dst, base, src, rows):
    for j in range(SUB):
        dst[pl.ds(base * SUB + j, rows, stride=SUB), :] = src[:, j * LANES : (j + 1) * LANES]


def local_kernel(
    length, proj, rim, taps, rates, residues, skip, state_out, base_out, query_out, xs, tap_s, mode_s
):
    rows = proj.shape[1]
    for g in range(3):
        spread(xs.at[g], 0, rim[g].astype(F32), RIM)
        spread(xs.at[g], RIM, proj[g].astype(F32), rows)
        spread(tap_s.at[g], 0, taps[g], TAPS)
    spread(mode_s.at[0], 0, jnp.exp(rates[...] * (-1.0 / length)), MODES)
    spread(mode_s.at[1], 0, residues[...] * (1.0 / math.sqrt(length)), MODES)

    def tile(ref, row):
        return ref[pl.ds(pl.multiple_of(row * SUB, SUB), SUB), :]

    group = 8

    def conv_step(step, carry):
        first = step * group
        done = []
        for g in range(3):
            window = [tile(xs.at[g], first + RIM - (TAPS - 1) + i) for i in range(group + TAPS - 1)]
            weights = [tile(tap_s.at[g], j) for j in range(TAPS)]
            outs = []
            for i in range(group):
                total = weights[0] * window[i + TAPS - 1]
                for j in range(1, TAPS):
                    total = total + weights[j] * window[i + TAPS - 1 - j]
                outs.append(total)
            done.append(outs)
        for i in range(group):
            query_out[first + i] = done[0][i]
            base_out[first + i] = (
                (done[1][i] * done[2][i]).astype(jnp.bfloat16).astype(F32)
            )
        return carry

    lax.fori_loop(0, rows // group, conv_step, 0)

    decay = [tile(mode_s.at[0], n) for n in range(MODES)]
    weight = [tile(mode_s.at[1], n) for n in range(MODES)]
    direct = skip[...]

    def scan_step(step, state):
        first = step * 4
        state = list(state)
        for i in range(4):
            kv = base_out[first + i]
            total = direct * kv
            for n in range(MODES):
                state[n] = decay[n] * state[n] + kv
            parts = [weight[n] * state[n] for n in range(MODES)]
            while len(parts) > 1:
                parts = [parts[k] + parts[k + 1] for k in range(0, len(parts), 2)]
            base_out[first + i] = total + parts[0]
        return tuple(state)

    zero = jnp.zeros((SUB, LANES), F32)
    state = lax.fori_loop(0, rows // 4, scan_step, (zero,) * MODES)
    for n in range(MODES):
        state_out[pl.ds(n, SUB, stride=MODES), :] = state[n]


def total_kernel(block, length, planes, states, rates, total_out):
    step = jnp.exp(rates[...] * (-float(block) / length))
    total = states[0]
    for p in range(1, PLANE):
        total = step * total + states[p]
    total = total.astype(total_out.dtype)
    for z in range(planes):
        total_out[z] = total


def carry_kernel(block, length, planes, where, totals, states, rates, carry_out):
    mine = where[0]
    rate = rates[...]
    carry = jnp.zeros((MODES, LANES), F32)
    for z in range(planes):
        gap = jnp.maximum(mine - 1 - z, 0).astype(F32) * (float(block * PLANE) / length)
        share = jnp.exp(-(rate * gap)) * totals[z].astype(F32)
        carry = carry + jnp.where(z < mine, share, 0.0)
    step = jnp.exp(rate * (-float(block) / length))
    for p in range(PLANE):
        carry_out[p] = carry
        carry = step * carry + states[p]


def gate_kernel(
    length, carry, rates, residues, base, query, gated_out, squares_out, mode_s, tiles
):
    rows = base.shape[0]
    spread(mode_s.at[0], 0, jnp.exp(rates[...] * (-1.0 / length)), MODES)
    spread(mode_s.at[1], 0, residues[...] * (1.0 / math.sqrt(length)), MODES)

    def tile(ref, row):
        return ref[pl.ds(pl.multiple_of(row * SUB, SUB), SUB), :]

    decay = [tile(mode_s.at[0], n) for n in range(MODES)]
    start = tuple(
        decay[n] * tile(mode_s.at[1], n) * carry[pl.ds(n, SUB, stride=MODES), :]
        for n in range(MODES)
    )

    def step_fn(step, state):
        first = step * 4
        state = list(state)
        for i in range(4):
            parts = list(state)
            while len(parts) > 1:
                parts = [parts[k] + parts[k + 1] for k in range(0, len(parts), 2)]
            value = query[first + i] * (base[first + i] + parts[0])
            tiles[pl.ds(pl.multiple_of((first + i) * SUB, SUB), SUB), :] = value
            state = [decay[n] * state[n] for n in range(MODES)]
        return tuple(state)

    lax.fori_loop(0, rows // 4, step_fn, start)
    squares = jnp.zeros((rows, LANES), F32)
    for j in range(SUB):
        part = tiles[pl.ds(j, rows, stride=SUB), :]
        gated_out[:, j * LANES : (j + 1) * LANES] = part
        squares = squares + part * part
    ones = jnp.ones((SUB, LANES), F32)
    line = lax.dot_general(
        ones, squares, (((1,), (1,)), ((), ())), precision=HIGHEST, preferred_element_type=F32
    )
    squares_out[...] = line[: squares_out.shape[0]]


def norm_kernel(width, gated, squares, gain, out):
    count = squares.shape[0]
    ones = jnp.ones((count, LANES), F32)
    total = lax.dot_general(
        squares[...], ones, (((0,), (0,)), ((), ())), precision=HIGHEST, preferred_element_type=F32
    )
    scale = lax.rsqrt(total * (1.0 / width) + 1e-05)
    for j in range(SUB):
        cols = slice(j * LANES, (j + 1) * LANES)
        out[:, cols] = (gated[:, cols] * gain[:, cols] * scale).astype(out.dtype)


def shards(projected, short_taps, residues, rates, skip_gain, norm_gain):
    rows = projected.shape[0]
    channels = projected.shape[2]
    groups = lax.axis_size("ctx")
    parts = lax.axis_size("tp")
    planes = groups // PLANE
    length = rows * groups
    me = lax.axis_index("ctx")
    in_plane = [[z * PLANE + p for p in range(PLANE)] for z in range(planes)]
    along_z = [[z * PLANE + p for z in range(planes)] for p in range(PLANE)]

    proj = jnp.transpose(projected, (1, 0, 2))
    rate_t = rates.T
    residue_t = residues.T
    rim = lax.ppermute(
        proj[:, rows - RIM :], "ctx", [(i, i + 1) for i in range(groups - 1)]
    )
    own_rates = lax.dynamic_slice_in_dim(rate_t, (me % PLANE) * LANES, LANES, 1)
    plane_at = (me // PLANE).astype(jnp.int32).reshape(1)

    states, base, query = pl.pallas_call(
        lambda *refs: local_kernel(length, *refs),
        name="local",
        out_shape=(
            jax.ShapeDtypeStruct((SUB * MODES, LANES), F32),
            jax.ShapeDtypeStruct((rows, SUB, LANES), F32),
            jax.ShapeDtypeStruct((rows, SUB, LANES), F32),
        ),
        in_specs=[whole()] * 6,
        out_specs=(whole(),) * 3,
        scratch_shapes=[
            pltpu.VMEM((3, (RIM + rows) * SUB, LANES), F32),
            pltpu.VMEM((3, TAPS * SUB, LANES), F32),
            pltpu.VMEM((2, MODES * SUB, LANES), F32),
        ],
        compiler_params=pltpu.CompilerParams(vmem_limit_bytes=32 << 20),
    )(proj, rim, short_taps, rate_t, residue_t, skip_gain.reshape(SUB, LANES))

    met = lax.all_to_all(
        states.reshape(SUB, MODES, LANES), "ctx", 0, 0, tiled=True, axis_index_groups=in_plane
    )
    totals = pl.pallas_call(
        lambda *refs: total_kernel(rows, length, planes, *refs),
        name="total",
        out_shape=jax.ShapeDtypeStruct((planes, MODES, LANES), jnp.bfloat16),
        in_specs=[whole()] * 2,
        out_specs=whole(),
    )(met, own_rates)
    gathered = lax.all_to_all(totals, "ctx", 0, 0, tiled=True, axis_index_groups=along_z)
    carries = pl.pallas_call(
        lambda *refs: carry_kernel(rows, length, planes, *refs),
        name="carry",
        out_shape=jax.ShapeDtypeStruct((PLANE, MODES, LANES), F32),
        in_specs=[whole(pltpu.SMEM)] + [whole()] * 3,
        out_specs=whole(),
    )(plane_at, gathered, met, own_rates)
    carry = lax.all_to_all(carries, "ctx", 0, 0, tiled=True, axis_index_groups=in_plane)

    gated, squares = pl.pallas_call(
        lambda *refs: gate_kernel(length, *refs),
        name="gate",
        out_shape=(
            jax.ShapeDtypeStruct((rows, channels), F32),
            jax.ShapeDtypeStruct((parts, rows), F32),
        ),
        in_specs=[whole()] * 5,
        out_specs=(whole(),) * 2,
        scratch_shapes=[
            pltpu.VMEM((2, MODES * SUB, LANES), F32),
            pltpu.VMEM((rows * SUB, LANES), F32),
        ],
        compiler_params=pltpu.CompilerParams(vmem_limit_bytes=32 << 20),
    )(carry.reshape(SUB * MODES, LANES), rate_t, residue_t, base, query)
    squares = lax.all_to_all(squares, "tp", 0, 0, tiled=True)
    return pl.pallas_call(
        lambda *refs: norm_kernel(channels * parts, *refs),
        name="norm",
        out_shape=jax.ShapeDtypeStruct((rows, channels), jnp.bfloat16),
        in_specs=[whole()] * 3,
        out_specs=whole(),
    )(gated, squares, norm_gain.reshape(1, channels))


def solution(mesh):
    return jax.shard_map(
        shards,
        mesh=mesh,
        in_specs=(
            P("ctx", None, "tp"),
            P(None, None, "tp"),
            P("tp", None),
            P("tp", None),
            P("tp"),
            P("tp"),
        ),
        out_specs=P("ctx", "tp"),
        check_vma=False,
    )
```

```python
import math

import jax
import jax.numpy as jnp
from jax import lax
from jax.experimental import pallas as pl
from jax.experimental.pallas import tpu as pltpu
from jax.sharding import PartitionSpec as P

TAPS = 7
MODES = 16
LANES = 128
SUB = 8
PLANE = 8
HEAD = 8
GROUP = 8
HIGHEST = lax.Precision.HIGHEST
F32 = jnp.float32


def whole(memory_space=pltpu.VMEM):
    return pl.BlockSpec(memory_space=memory_space)


def spread(dst, base, src, rows):
    for j in range(SUB):
        dst[pl.ds(base * SUB + j, rows, stride=SUB), :] = src[:, j * LANES : (j + 1) * LANES]


def tile(ref, row):
    return ref[pl.ds(pl.multiple_of(row * SUB, SUB), SUB), :]


def tree_sum(parts):
    while len(parts) > 1:
        parts = [parts[k] + parts[k + 1] for k in range(0, len(parts), 2)]
    return parts[0]


def spread_modes(mode_s, rates, residues, length):
    spread(mode_s.at[0], 0, jnp.exp(rates[...] * (-1.0 / length)), MODES)
    spread(mode_s.at[1], 0, residues[...] * (1.0 / math.sqrt(length)), MODES)


def short_convs(xs, tap_s, first, base_out, query_out, at):
    done = []
    for g in range(3):
        window = [tile(xs.at[g], first - (TAPS - 1) + i) for i in range(GROUP + TAPS - 1)]
        weights = [tile(tap_s.at[g], j) for j in range(TAPS)]
        outs = []
        for i in range(GROUP):
            total = weights[0] * window[i + TAPS - 1]
            for j in range(1, TAPS):
                total = total + weights[j] * window[i + TAPS - 1 - j]
            outs.append(total)
        done.append(outs)
    for i in range(GROUP):
        query_out[at + i] = done[0][i]
        base_out[at + i] = (done[1][i] * done[2][i]).astype(jnp.bfloat16).astype(F32)


def scan(first, count, decay, weight, direct, state, base_out):
    state = list(state)
    for i in range(count):
        kv = base_out[first + i]
        state = [decay[n] * state[n] + kv for n in range(MODES)]
        base_out[first + i] = direct * kv + tree_sum(
            [weight[n] * state[n] for n in range(MODES)]
        )
    return tuple(state)


def rest_kernel(
    length, proj, taps, rates, residues, skip, state_out, base_out, query_out, xs, tap_s, mode_s
):
    rows = proj.shape[1]
    for g in range(3):
        spread(xs.at[g], 0, proj[g].astype(F32), rows)
        spread(tap_s.at[g], 0, taps[g], TAPS)
    spread_modes(mode_s, rates, residues, length)

    def conv_step(step, nothing):
        at = step * GROUP
        short_convs(xs, tap_s, at + HEAD, base_out, query_out, at)
        return nothing

    lax.fori_loop(0, (rows - HEAD) // GROUP, conv_step, 0)
    decay = [tile(mode_s.at[0], n) for n in range(MODES)]
    weight = [tile(mode_s.at[1], n) for n in range(MODES)]
    direct = skip[...]

    def scan_step(step, state):
        return scan(step * 4, 4, decay, weight, direct, state, base_out)

    zero = jnp.zeros((SUB, LANES), F32)
    state = lax.fori_loop(0, (rows - HEAD) // 4, scan_step, (zero,) * MODES)
    for n in range(MODES):
        state_out[n] = state[n]


def head_kernel(
    length,
    block,
    rim,
    proj,
    taps,
    rates,
    residues,
    skip,
    rest,
    state_out,
    enter_out,
    base_out,
    query_out,
    xs,
    tap_s,
    mode_s,
    fade_s,
):
    for g in range(3):
        spread(xs.at[g], 0, rim[g].astype(F32), HEAD)
        spread(xs.at[g], HEAD, proj[g].astype(F32)[:HEAD], HEAD)
        spread(tap_s.at[g], 0, taps[g], TAPS)
    spread_modes(mode_s, rates, residues, length)
    spread(fade_s, 0, jnp.exp(rates[...] * (-float(block - HEAD) / length)), MODES)
    short_convs(xs, tap_s, HEAD, base_out, query_out, 0)
    decay = [tile(mode_s.at[0], n) for n in range(MODES)]
    weight = [tile(mode_s.at[1], n) for n in range(MODES)]
    zero = jnp.zeros((SUB, LANES), F32)
    state = scan(0, HEAD, decay, weight, skip[...], (zero,) * MODES, base_out)
    for n in range(MODES):
        enter_out[n] = decay[n] * weight[n] * state[n]
        state_out[pl.ds(n, SUB, stride=MODES), :] = rest[n] + tile(fade_s, n) * state[n]


def own_columns(rates):
    at = lax.rem(lax.axis_index("ctx"), PLANE)
    return rates[:, pl.ds(pl.multiple_of(at * LANES, LANES), LANES)]


def total_kernel(block, length, planes, states, rates, total_out):
    step = jnp.exp(own_columns(rates) * (-float(block) / length))
    total = states[0]
    for p in range(1, PLANE):
        total = step * total + states[p]
    total = total.astype(total_out.dtype)
    for z in range(planes):
        total_out[z] = total


def carry_kernel(block, length, planes, totals, states, rates, carry_out):
    mine = lax.div(lax.axis_index("ctx"), PLANE)
    rate = own_columns(rates)
    carry = jnp.zeros((MODES, LANES), F32)
    for z in range(planes):
        gap = jnp.maximum(mine - 1 - z, 0).astype(F32) * (float(block * PLANE) / length)
        share = jnp.exp(-(rate * gap)) * totals[z].astype(F32)
        carry = carry + jnp.where(z < mine, share, 0.0)
    step = jnp.exp(rate * (-float(block) / length))
    for p in range(PLANE):
        carry_out[p] = carry
        carry = step * carry + states[p]


def gate_kernel(
    length,
    carry,
    rates,
    residues,
    enter,
    base_head,
    query_head,
    base,
    query,
    gated_out,
    squares_out,
    mode_s,
    tiles,
):
    rows = HEAD + base.shape[0]
    spread_modes(mode_s, rates, residues, length)
    decay = [tile(mode_s.at[0], n) for n in range(MODES)]
    state = [
        decay[n] * tile(mode_s.at[1], n) * carry[pl.ds(n, SUB, stride=MODES), :]
        for n in range(MODES)
    ]

    def four(first, base, query, at, state):
        for i in range(4):
            value = query[first + i] * (base[first + i] + tree_sum(list(state)))
            tiles[pl.ds(pl.multiple_of((at + i) * SUB, SUB), SUB), :] = value
            state = [decay[n] * state[n] for n in range(MODES)]
        return tuple(state)

    for at in range(0, HEAD, 4):
        state = four(at, base_head, query_head, at, state)
    state = tuple(state[n] + enter[n] for n in range(MODES))
    lax.fori_loop(
        0,
        (rows - HEAD) // 4,
        lambda step, held: four(step * 4, base, query, step * 4 + HEAD, held),
        state,
    )
    squares = jnp.zeros((rows, LANES), F32)
    for j in range(SUB):
        part = tiles[pl.ds(j, rows, stride=SUB), :]
        gated_out[:, j * LANES : (j + 1) * LANES] = part
        squares = squares + part * part
    ones = jnp.ones((SUB, LANES), F32)
    line = lax.dot_general(
        ones, squares, (((1,), (1,)), ((), ())), precision=HIGHEST, preferred_element_type=F32
    )
    squares_out[...] = line[: squares_out.shape[0]]


def norm_kernel(width, gated, squares, gain, out):
    count = squares.shape[0]
    ones = jnp.ones((count, LANES), F32)
    total = lax.dot_general(
        squares[...], ones, (((0,), (0,)), ((), ())), precision=HIGHEST, preferred_element_type=F32
    )
    scale = lax.rsqrt(total * (1.0 / width) + 1e-05)
    for j in range(SUB):
        cols = slice(j * LANES, (j + 1) * LANES)
        out[:, cols] = (gated[:, cols] * gain[:, cols] * scale).astype(out.dtype)


def on_chip(mebibytes):
    return pltpu.CompilerParams(vmem_limit_bytes=mebibytes << 20)


def array(*shape):
    return jax.ShapeDtypeStruct(shape, F32)


def shards(projected, short_taps, residues, rates, skip_gain, norm_gain):
    rows = projected.shape[0]
    channels = projected.shape[2]
    groups = lax.axis_size("ctx")
    parts = lax.axis_size("tp")
    planes = groups // PLANE
    length = rows * groups
    in_plane = [[z * PLANE + p for p in range(PLANE)] for z in range(planes)]
    along_z = [[z * PLANE + p for z in range(planes)] for p in range(PLANE)]

    proj = jnp.transpose(projected, (1, 0, 2))
    rate_t = rates.T
    residue_t = residues.T
    skip = skip_gain.reshape(SUB, LANES)
    rim = lax.ppermute(
        proj[:, rows - HEAD :], "ctx", [(i, i + 1) for i in range(groups - 1)]
    )
    tap_tiles = pltpu.VMEM((3, TAPS * SUB, LANES), F32)
    mode_tiles = pltpu.VMEM((2, MODES * SUB, LANES), F32)
    rest, base, query = pl.pallas_call(
        lambda *refs: rest_kernel(length, *refs),
        name="rest",
        out_shape=(
            array(MODES, SUB, LANES),
            array(rows - HEAD, SUB, LANES),
            array(rows - HEAD, SUB, LANES),
        ),
        in_specs=[whole()] * 5,
        out_specs=(whole(),) * 3,
        scratch_shapes=[pltpu.VMEM((3, rows * SUB, LANES), F32), tap_tiles, mode_tiles],
        compiler_params=on_chip(16),
        cost_estimate=pl.CostEstimate(
            flops=100 * rows * channels, bytes_accessed=4 << 20, transcendentals=0
        ),
    )(proj, short_taps, rate_t, residue_t, skip)
    states, enter, base_head, query_head = pl.pallas_call(
        lambda *refs: head_kernel(length, rows, *refs),
        name="head",
        out_shape=(
            array(SUB * MODES, LANES),
            array(MODES, SUB, LANES),
            array(HEAD, SUB, LANES),
            array(HEAD, SUB, LANES),
        ),
        grid=(1,),
        in_specs=[
            whole(),
            pl.BlockSpec((3, 16, channels), lambda i: (0, 0, 0)),
        ]
        + [whole()] * 5,
        out_specs=(whole(),) * 4,
        scratch_shapes=[
            pltpu.VMEM((3, 2 * HEAD * SUB, LANES), F32),
            tap_tiles,
            mode_tiles,
            pltpu.VMEM((MODES * SUB, LANES), F32),
        ],
        compiler_params=on_chip(8),
    )(rim, proj, short_taps, rate_t, residue_t, skip, rest)

    met = lax.all_to_all(
        states.reshape(SUB, MODES, LANES), "ctx", 0, 0, tiled=True, axis_index_groups=in_plane
    )
    totals = pl.pallas_call(
        lambda *refs: total_kernel(rows, length, planes, *refs),
        name="total",
        out_shape=jax.ShapeDtypeStruct((planes, MODES, LANES), jnp.bfloat16),
        in_specs=[whole()] * 2,
        out_specs=whole(),
        compiler_params=on_chip(4),
    )(met, rate_t)
    gathered = lax.all_to_all(totals, "ctx", 0, 0, tiled=True, axis_index_groups=along_z)
    carries = pl.pallas_call(
        lambda *refs: carry_kernel(rows, length, planes, *refs),
        name="carry",
        out_shape=array(PLANE, MODES, LANES),
        in_specs=[whole()] * 3,
        out_specs=whole(),
        compiler_params=on_chip(4),
    )(gathered, met, rate_t)
    carry = lax.all_to_all(carries, "ctx", 0, 0, tiled=True, axis_index_groups=in_plane)

    gated, squares = pl.pallas_call(
        lambda *refs: gate_kernel(length, *refs),
        name="gate",
        out_shape=(array(rows, channels), array(parts, rows)),
        in_specs=[whole()] * 8,
        out_specs=(whole(),) * 2,
        scratch_shapes=[mode_tiles, pltpu.VMEM((rows * SUB, LANES), F32)],
        compiler_params=on_chip(16),
    )(
        carry.reshape(SUB * MODES, LANES),
        rate_t,
        residue_t,
        enter,
        base_head,
        query_head,
        base,
        query,
    )
    squares = lax.all_to_all(squares, "tp", 0, 0, tiled=True)
    return pl.pallas_call(
        lambda *refs: norm_kernel(channels * parts, *refs),
        name="norm",
        out_shape=jax.ShapeDtypeStruct((rows, channels), jnp.bfloat16),
        in_specs=[whole()] * 3,
        out_specs=whole(),
        compiler_params=on_chip(4),
    )(gated, squares, norm_gain.reshape(1, channels))


def solution(mesh):
    return jax.shard_map(
        shards,
        mesh=mesh,
        in_specs=(
            P("ctx", None, "tp"),
            P(None, None, "tp"),
            P("tp", None),
            P("tp", None),
            P("tp"),
            P("tp"),
        ),
        out_specs=P("ctx", "tp"),
        check_vma=False,
    )
```

```python
import math

import jax
import jax.numpy as jnp
from jax import lax
from jax.experimental import pallas as pl
from jax.experimental.pallas import tpu as pltpu
from jax.sharding import PartitionSpec as P

TAPS = 7
MODES = 16
LANES = 128
SUB = 8
OWNERS = 16
HALF = LANES // 2
HEAD = 8
GROUP = 8
FIRST, LAST, SENT = 8, 16, 32
BACK = 24
TAP_AT = 3 * HEAD
DECAY_AT = TAP_AT + 3 * TAPS
WEIGHT_AT = DECAY_AT + MODES
SKIP_AT = WEIGHT_AT + MODES
KEPT = SKIP_AT + 1
EARLY = 2
HIGHEST = lax.Precision.HIGHEST
F32 = jnp.float32
BF16 = jnp.bfloat16


def whole(memory_space=pltpu.VMEM):
    return pl.BlockSpec(memory_space=memory_space)


def spread(dst, base, src, rows):
    for j in range(SUB):
        dst[pl.ds(base * SUB + j, rows, stride=SUB), :] = src[:, j * LANES : (j + 1) * LANES]


def tile(ref, row):
    return ref[pl.ds(pl.multiple_of(row * SUB, SUB), SUB), :]


def tree_sum(parts):
    while len(parts) > 1:
        parts = [parts[k] + parts[k + 1] for k in range(0, len(parts), 2)]
    return parts[0]


def swap(x):
    return pltpu.roll(x, HALF, 1)


def paired(first, second):
    low = lax.broadcasted_iota(jnp.int32, first.shape, 1) < HALF
    return jnp.where(low, first, swap(second)), jnp.where(low, swap(first), second)


def short_conv(xs, kept, g, first):
    window = [tile(xs, first - (TAPS - 1) + i) for i in range(GROUP + TAPS - 1)]
    weights = [tile(kept, TAP_AT + g * TAPS + j) for j in range(TAPS)]
    outs = []
    for i in range(GROUP):
        total = weights[0] * window[i + TAPS - 1]
        for j in range(1, TAPS):
            total = total + weights[j] * window[i + TAPS - 1 - j]
        outs.append(total)
    return outs


def products(keys, values):
    return [(k * v).astype(BF16).astype(F32) for k, v in zip(keys, values)]


def constants(kept):
    decay = [tile(kept, DECAY_AT + n) for n in range(MODES)]
    weight = [tile(kept, WEIGHT_AT + n) for n in range(MODES)]
    return decay, weight, tile(kept, SKIP_AT)


def advance(first, count, decay, state, source):
    state = list(state)
    for i in range(count):
        kv = source[first + i]
        state = [decay[n] * state[n] + kv for n in range(MODES)]
    return tuple(state)


def scan(first, count, decay, weight, direct, state, source, dest):
    state = list(state)
    for i in range(count):
        kv = source[first + i]
        state = [decay[n] * state[n] + kv for n in range(MODES)]
        dest[first + i] = direct * kv + tree_sum([weight[n] * state[n] for n in range(MODES)])
    return tuple(state)


def nothing():
    return (jnp.zeros((SUB, LANES), F32),) * MODES


def is_early():
    return lax.axis_index("ctx") < EARLY * OWNERS


def local_kernel(
    length,
    proj_hbm,
    taps_hbm,
    rates_hbm,
    residues_hbm,
    skip_hbm,
    message_out,
    base_out,
    query_out,
    kept,
    proj,
    taps,
    rates,
    residues,
    xs,
    state_s,
    rows_s,
    arrived,
):
    pieces = [(proj_hbm.at[g], proj.at[g]) for g in (1, 2, 0)]
    pieces[2:2] = [
        (taps_hbm, taps),
        (rates_hbm, rates),
        (residues_hbm, residues),
        (skip_hbm, kept.at[pl.ds(SKIP_AT * SUB, SUB)]),
    ]
    copies = [
        pltpu.make_async_copy(src, dst, arrived.at[i]) for i, (src, dst) in enumerate(pieces)
    ]
    for copy in copies:
        copy.start()
    rows = proj.shape[1]
    for g, copy in ((1, copies[0]), (2, copies[1])):
        copy.wait()
        spread(xs.at[g], 0, proj[g].astype(F32), rows)
    for copy in copies[2:6]:
        copy.wait()
    for g in range(3):
        spread(kept, TAP_AT + g * TAPS, taps[g], TAPS)
    spread(kept, DECAY_AT, jnp.exp(rates[...] * (-1.0 / length)), MODES)
    spread(kept, WEIGHT_AT, residues[...] * (1.0 / math.sqrt(length)), MODES)
    copies[6].wait()
    spread(xs.at[0], 0, proj[0].astype(F32), rows)
    for g in range(3):
        kept[pl.ds(g * HEAD * SUB, HEAD * SUB), :] = xs[g, : HEAD * SUB, :]
    decay, weight, direct = constants(kept)

    def conv_step(step, early):
        at = step * GROUP
        kv = products(*(short_conv(xs.at[g], kept, g, at + HEAD) for g in (1, 2)))
        if early:
            query = short_conv(xs.at[0], kept, 0, at + HEAD)
        else:
            query = [tile(xs.at[0], at + HEAD + i) for i in range(GROUP)]
        for i in range(GROUP):
            base_out[at + i] = kv[i]
            query_out[at + i] = query[i]

    def finish(early):
        def conv(step, carried):
            conv_step(step, early)
            return carried

        def step_fn(step, state):
            if early:
                return scan(step * 4, 4, decay, weight, direct, state, base_out, base_out)
            return advance(step * 4, 4, decay, state, base_out)

        lax.fori_loop(0, (rows - HEAD) // GROUP, conv, 0)
        state = lax.fori_loop(0, (rows - HEAD) // 4, step_fn, nothing())
        for n in range(MODES):
            state_s[n] = state[n]

    early = is_early()
    pl.when(early)(lambda: finish(True))
    pl.when(jnp.logical_not(early))(lambda: finish(False))

    for n in range(SUB):
        for h, value in enumerate(paired(state_s[n], state_s[n + SUB])):
            rows_s[pl.ds(h * SENT + n, SUB, stride=2 * SENT), :] = value
    for j in range(SUB):
        cols = slice(j * LANES, (j + 1) * LANES)
        ends = [proj[g, rows - 16 :, cols].astype(F32)[16 - HEAD :] for g in range(3)]
        starts = [proj[g, :16, cols].astype(F32)[:HEAD] for g in range(3)]
        for at, (first, second) in (
            (FIRST, (starts[1], starts[2])),
            (LAST, (ends[1], ends[2])),
            (LAST + HEAD, (ends[0], ends[0])),
        ):
            for h, value in enumerate(paired(first, second)):
                rows_s[pl.ds((2 * j + h) * SENT + at, HEAD), :] = value
    for d in range(OWNERS):
        message_out[d] = rows_s[pl.ds(d * SENT, SENT), :].astype(BF16)


def owned(source, rows, row_s):
    spot = lax.rem(lax.axis_index("ctx"), OWNERS)
    lanes = pl.ds(pl.multiple_of(lax.div(spot, 2) * LANES, LANES), LANES)
    first, second = source(lanes)
    row_s[0, :rows] = first
    row_s[1, :rows] = second
    lower, upper = paired(row_s[0], row_s[1])
    return jnp.where(lax.rem(spot, 2) == 0, lower, upper)


def own_rates(rates, row_s):
    return owned(lambda lanes: (rates[:SUB, lanes], rates[SUB:, lanes]), SUB, row_s)


def own_taps(taps, row_s):
    return owned(lambda lanes: (taps[1, :, lanes], taps[2, :, lanes]), TAPS, row_s)


def edge_state(before, first, taps, fades):
    window = jnp.concatenate([before, first], 0)
    conv = taps[0:1] * first
    for j in range(1, TAPS):
        conv = conv + taps[j : j + 1] * window[HEAD - j : 2 * HEAD - j]
    product = (conv * swap(conv)).astype(BF16).astype(F32)
    total = fades[0] * product[0:1]
    for s in range(1, HEAD):
        total = total + fades[s] * product[s : s + 1]
    return total


def edge_fades(rate, block, length):
    return [jnp.exp(rate * (-float(block - 1 - s) / length)) for s in range(HEAD)]


def meet_kernel(block, length, teams, met, rates, taps, states_out, sent_out, row_s):
    rate = own_rates(rates, row_s)
    weights = own_taps(taps, row_s)
    fades = edge_fades(rate, block, length)
    step = jnp.exp(rate * (-float(block) / length))
    total = None
    before = None
    for d in range(OWNERS):
        rows = met[d].astype(F32)
        state = rows[:SUB]
        if d:
            state = state + edge_state(before, rows[FIRST : FIRST + HEAD], weights, fades)
        states_out[d] = state
        total = state if d == 0 else step * total + state
        before = rows[LAST : LAST + HEAD]
    ending = met[OWNERS - 1].astype(F32)[LAST:].astype(BF16)
    opening = met[0].astype(F32)[FIRST : FIRST + HEAD]
    beginning = jnp.concatenate([total, opening], 0).astype(BF16)
    for m in range(teams):
        sent_out[m, :16] = ending
        sent_out[m, 16:] = beginning


def carry_kernel(
    block, length, teams, gathered, states, met, rates, taps, kept, back_out, row_s, edge_s
):
    del kept
    mine = lax.div(lax.axis_index("ctx"), OWNERS)
    rate = own_rates(rates, row_s)
    weights = own_taps(taps, row_s)
    fades = edge_fades(rate, block, length)
    whole_team = float(block * OWNERS) / length
    to_end = jnp.exp(rate * (-float(block * (OWNERS - 1)) / length))
    carry = jnp.zeros((SUB, LANES), F32)
    before = jnp.zeros((HEAD, LANES), F32)
    edge_s[0, :HEAD] = before
    edge_s[0, HEAD : 2 * HEAD] = before
    for m in range(teams):
        rows = gathered[m].astype(F32)
        edge = edge_state(before, rows[24:], weights, fades)
        edge_s[m, 2 * HEAD :] = edge
        gap = jnp.maximum(mine - 1 - m, 0).astype(F32) * whole_team
        share = jnp.exp(-(rate * gap)) * (rows[16:24] + to_end * edge)
        carry = carry + jnp.where(m < mine, share, 0.0)
        before = rows[:HEAD]
        if m + 1 < teams:
            edge_s[m + 1, : 2 * HEAD] = rows[: 2 * HEAD]
    step = jnp.exp(rate * (-float(block) / length))
    here = edge_s[mine]
    for d in range(OWNERS):
        if d == 0:
            ahead = here[: 2 * HEAD]
        else:
            ahead = met[d - 1].astype(F32)[LAST:]
        back_out[d] = jnp.concatenate([carry, ahead], 0).astype(BF16)
        state = states[d]
        if d == 0:
            state = state + here[2 * HEAD :]
        carry = step * carry + state


def gate_kernel(
    back,
    kept,
    base,
    query,
    gated_out,
    squares_out,
    xs,
    base_head,
    query_head,
    rows_s,
    tiles,
    raw_s,
    base_s,
    query_s,
):
    rest = base.shape[0]
    rows = HEAD + rest
    for g in range(3):
        xs[g, HEAD * SUB :] = kept[pl.ds(g * HEAD * SUB, HEAD * SUB), :]
    for d in range(OWNERS):
        rows_s[pl.ds(d * BACK, BACK), :] = back[d].astype(F32)

    def received(row):
        return paired(
            rows_s[pl.ds(row, SUB, stride=2 * BACK), :],
            rows_s[pl.ds(BACK + row, SUB, stride=2 * BACK), :],
        )

    for r in range(HEAD):
        key, value = received(SUB + r)
        xs[1, r * SUB : (r + 1) * SUB] = key
        xs[2, r * SUB : (r + 1) * SUB] = value
        xs[0, r * SUB : (r + 1) * SUB] = received(SUB + HEAD + r)[0]
    kv = products(*(short_conv(xs.at[g], kept, g, HEAD) for g in (1, 2)))
    for i, value in enumerate(short_conv(xs.at[0], kept, 0, HEAD)):
        query_head[i] = value
        base_head[i] = kv[i]
    decay, weight, direct = constants(kept)
    entered = scan(0, HEAD, decay, weight, direct, nothing(), base_head, base_head)
    state = [None] * MODES
    for n in range(SUB):
        for value, m in zip(received(n), (n, n + SUB)):
            state[m] = decay[m] * weight[m] * value

    def four(first, base, query, at, state):
        for i in range(4):
            value = query[first + i] * (base[first + i] + tree_sum(list(state)))
            tiles[pl.ds(pl.multiple_of((at + i) * SUB, SUB), SUB), :] = value
            state = [decay[n] * state[n] for n in range(MODES)]
        return tuple(state)

    for at in range(0, HEAD, 4):
        state = four(at, base_head, query_head, at, state)
    state = tuple(state[n] + decay[n] * weight[n] * entered[n] for n in range(MODES))

    def apply(base, query):
        lax.fori_loop(
            0,
            rest // 4,
            lambda step, held: four(step * 4, base, query, step * 4 + HEAD, held),
            state,
        )

    def own_output():
        raw_s[: HEAD * SUB] = xs[0, HEAD * SUB :]

        def lay(step, carried):
            for i in range(GROUP):
                row = step * GROUP + i
                raw_s[pl.ds(pl.multiple_of((row + HEAD) * SUB, SUB), SUB), :] = query[row]
            return carried

        def conv(step, carried):
            at = step * GROUP
            for i, value in enumerate(short_conv(raw_s, kept, 0, at + HEAD)):
                query_s[at + i] = value
            return carried

        lax.fori_loop(0, rest // GROUP, lay, 0)
        lax.fori_loop(0, rest // GROUP, conv, 0)
        lax.fori_loop(
            0,
            rest // 4,
            lambda step, held: scan(step * 4, 4, decay, weight, direct, held, base, base_s),
            nothing(),
        )
        apply(base_s, query_s)

    early = is_early()
    pl.when(early)(lambda: apply(base, query))
    pl.when(jnp.logical_not(early))(own_output)
    squares = jnp.zeros((rows, LANES), F32)
    for j in range(SUB):
        part = tiles[pl.ds(j, rows, stride=SUB), :]
        gated_out[:, j * LANES : (j + 1) * LANES] = part
        squares = squares + part * part
    ones = jnp.ones((SUB, LANES), F32)
    line = lax.dot_general(
        ones, squares, (((1,), (1,)), ((), ())), precision=HIGHEST, preferred_element_type=F32
    )
    squares_out[...] = line[: squares_out.shape[0]]


def norm_kernel(width, gated, squares, gain, out):
    count = squares.shape[0]
    ones = jnp.ones((count, LANES), F32)
    total = lax.dot_general(
        squares[...], ones, (((0,), (0,)), ((), ())), precision=HIGHEST, preferred_element_type=F32
    )
    scale = lax.rsqrt(total * (1.0 / width) + 1e-05)
    for j in range(SUB):
        cols = slice(j * LANES, (j + 1) * LANES)
        out[:, cols] = (gated[:, cols] * gain[:, cols] * scale).astype(out.dtype)


def on_chip(mebibytes):
    return pltpu.CompilerParams(vmem_limit_bytes=mebibytes << 20)


def array(*shape):
    return jax.ShapeDtypeStruct(shape, F32)


def shards(projected, short_taps, residues, rates, skip_gain, norm_gain):
    rows = projected.shape[0]
    channels = projected.shape[2]
    groups = lax.axis_size("ctx")
    parts = lax.axis_size("tp")
    teams = groups // OWNERS
    length = rows * groups
    in_team = [[m * OWNERS + d for d in range(OWNERS)] for m in range(teams)]
    across = [[m * OWNERS + d for m in range(teams)] for d in range(OWNERS)]

    proj = jnp.transpose(projected, (1, 0, 2))
    rate_t = rates.T
    residue_t = residues.T
    skip = skip_gain.reshape(SUB, LANES)
    block_tiles = pltpu.VMEM((rows - HEAD, SUB, LANES), F32)
    head_tiles = pltpu.VMEM((HEAD, SUB, LANES), F32)
    row_pair = pltpu.VMEM((2, SUB, LANES), F32)
    inputs = (proj, short_taps, rate_t, residue_t, skip)
    message, base, query, kept = pl.pallas_call(
        lambda *refs: local_kernel(length, *refs),
        name="local",
        out_shape=(
            jax.ShapeDtypeStruct((OWNERS, SENT, LANES), BF16),
            array(rows - HEAD, SUB, LANES),
            array(rows - HEAD, SUB, LANES),
            array(KEPT * SUB, LANES),
        ),
        in_specs=[whole(pltpu.HBM)] * 5,
        out_specs=(whole(),) * 4,
        scratch_shapes=[pltpu.VMEM(x.shape, x.dtype) for x in inputs[:4]]
        + [
            pltpu.VMEM((3, rows * SUB, LANES), F32),
            pltpu.VMEM((MODES, SUB, LANES), F32),
            pltpu.VMEM((OWNERS * SENT, LANES), F32),
            pltpu.SemaphoreType.DMA((7,)),
        ],
        compiler_params=on_chip(54),
    )(*inputs)

    met = lax.all_to_all(message, "ctx", 0, 0, tiled=True, axis_index_groups=in_team)
    states, sent = pl.pallas_call(
        lambda *refs: meet_kernel(rows, length, teams, *refs),
        name="meet",
        out_shape=(
            array(OWNERS, SUB, LANES),
            jax.ShapeDtypeStruct((teams, 4 * HEAD, LANES), BF16),
        ),
        in_specs=[whole()] * 3,
        out_specs=(whole(),) * 2,
        scratch_shapes=[row_pair],
        compiler_params=on_chip(4),
    )(met, rate_t, short_taps)
    gathered = lax.all_to_all(sent, "ctx", 0, 0, tiled=True, axis_index_groups=across)
    back = pl.pallas_call(
        lambda *refs: carry_kernel(rows, length, teams, *refs),
        name="carry",
        out_shape=jax.ShapeDtypeStruct((OWNERS, BACK, LANES), BF16),
        in_specs=[whole()] * 6,
        out_specs=whole(),
        scratch_shapes=[row_pair, pltpu.VMEM((teams, 3 * HEAD, LANES), F32)],
        compiler_params=on_chip(4),
    )(gathered, states, met, rate_t, short_taps, kept)
    back = lax.all_to_all(back, "ctx", 0, 0, tiled=True, axis_index_groups=in_team)

    gated, squares = pl.pallas_call(
        gate_kernel,
        name="gate",
        out_shape=(array(rows, channels), array(parts, rows)),
        in_specs=[whole()] * 4,
        out_specs=(whole(),) * 2,
        scratch_shapes=[
            pltpu.VMEM((3, 2 * HEAD * SUB, LANES), F32),
            head_tiles,
            head_tiles,
            pltpu.VMEM((OWNERS * BACK, LANES), F32),
            pltpu.VMEM((rows * SUB, LANES), F32),
            pltpu.VMEM((rows * SUB, LANES), F32),
            block_tiles,
            block_tiles,
        ],
        compiler_params=on_chip(16),
    )(back, kept, base, query)
    squares = lax.all_to_all(squares, "tp", 0, 0, tiled=True)
    return pl.pallas_call(
        lambda *refs: norm_kernel(channels * parts, *refs),
        name="norm",
        out_shape=jax.ShapeDtypeStruct((rows, channels), BF16),
        in_specs=[whole()] * 3,
        out_specs=whole(),
        compiler_params=on_chip(4),
    )(gated, squares, norm_gain.reshape(1, channels))


def solution(mesh):
    return jax.shard_map(
        shards,
        mesh=mesh,
        in_specs=(
            P("ctx", None, "tp"),
            P(None, None, "tp"),
            P("tp", None),
            P("tp", None),
            P("tp"),
            P("tp"),
        ),
        out_specs=P("ctx", "tp"),
        check_vma=False,
    )
```

```python
import math

import jax
import jax.numpy as jnp
from jax import lax
from jax.experimental import pallas as pl
from jax.experimental.pallas import tpu as pltpu
from jax.sharding import PartitionSpec as P

TAPS = 7
MODES = 16
LANES = 128
SUB = 8
OWNERS = 16
HALF = LANES // 2
HEAD = 8
GROUP = 8
FIRST, LAST, SENT = 8, 16, 32
BACK = 24
TAP_AT = 3 * HEAD
DECAY_AT = TAP_AT + 3 * TAPS
WEIGHT_AT = DECAY_AT + MODES
SKIP_AT = WEIGHT_AT + MODES
KEPT = SKIP_AT + 1
EARLY = 2
HIGHEST = lax.Precision.HIGHEST
F32 = jnp.float32
BF16 = jnp.bfloat16


def whole(memory_space=pltpu.VMEM):
    return pl.BlockSpec(memory_space=memory_space)


def spread(dst, base, src, rows):
    for j in range(SUB):
        dst[pl.ds(base * SUB + j, rows, stride=SUB), :] = src[:, j * LANES : (j + 1) * LANES]


def tile(ref, row):
    return ref[pl.ds(pl.multiple_of(row * SUB, SUB), SUB), :]


def tree_sum(parts):
    while len(parts) > 1:
        parts = [parts[k] + parts[k + 1] for k in range(0, len(parts), 2)]
    return parts[0]


def swap(x):
    return pltpu.roll(x, HALF, 1)


def paired(first, second):
    low = lax.broadcasted_iota(jnp.int32, first.shape, 1) < HALF
    return jnp.where(low, first, swap(second)), jnp.where(low, swap(first), second)


def short_conv(xs, kept, g, first):
    window = [tile(xs, first - (TAPS - 1) + i) for i in range(GROUP + TAPS - 1)]
    weights = [tile(kept, TAP_AT + g * TAPS + j) for j in range(TAPS)]
    outs = []
    for i in range(GROUP):
        total = weights[0] * window[i + TAPS - 1]
        for j in range(1, TAPS):
            total = total + weights[j] * window[i + TAPS - 1 - j]
        outs.append(total)
    return outs


def products(keys, values):
    return [(k * v).astype(BF16).astype(F32) for k, v in zip(keys, values)]


def constants(kept):
    decay = [tile(kept, DECAY_AT + n) for n in range(MODES)]
    weight = [tile(kept, WEIGHT_AT + n) for n in range(MODES)]
    return decay, weight, tile(kept, SKIP_AT)


def advance(first, count, decay, state, source):
    state = list(state)
    for i in range(count):
        kv = source[first + i]
        state = [decay[n] * state[n] + kv for n in range(MODES)]
    return tuple(state)


def scan(first, count, decay, weight, direct, state, source, dest):
    state = list(state)
    for i in range(count):
        kv = source[first + i]
        state = [decay[n] * state[n] + kv for n in range(MODES)]
        dest[first + i] = direct * kv + tree_sum([weight[n] * state[n] for n in range(MODES)])
    return tuple(state)


def nothing():
    return (jnp.zeros((SUB, LANES), F32),) * MODES


def is_early():
    return lax.axis_index("ctx") < EARLY * OWNERS


def local_kernel(
    length,
    proj_hbm,
    taps_hbm,
    rates_hbm,
    residues_hbm,
    skip_hbm,
    message_out,
    base_out,
    query_out,
    kept,
    raw_out,
    proj,
    taps,
    rates,
    residues,
    xs,
    state_s,
    rows_s,
    arrived,
):
    pieces = [
        (proj_hbm.at[1], proj.at[0]),
        (proj_hbm.at[2], proj.at[1]),
        (proj_hbm.at[0], raw_out),
    ]
    projections = (raw_out, proj.at[0], proj.at[1])
    pieces[2:2] = [
        (taps_hbm, taps),
        (rates_hbm, rates),
        (residues_hbm, residues),
        (skip_hbm, kept.at[pl.ds(SKIP_AT * SUB, SUB)]),
    ]
    copies = [
        pltpu.make_async_copy(src, dst, arrived.at[i]) for i, (src, dst) in enumerate(pieces)
    ]
    for copy in copies:
        copy.start()
    rows = raw_out.shape[0]
    for g, copy in ((1, copies[0]), (2, copies[1])):
        copy.wait()
        spread(xs.at[g], 0, projections[g][...].astype(F32), rows)
    for copy in copies[2:6]:
        copy.wait()
    for g in range(3):
        spread(kept, TAP_AT + g * TAPS, taps[g], TAPS)
    spread(kept, DECAY_AT, jnp.exp(rates[...] * (-1.0 / length)), MODES)
    spread(kept, WEIGHT_AT, residues[...] * (1.0 / math.sqrt(length)), MODES)
    copies[6].wait()
    early = is_early()
    spread(xs.at[0], 0, raw_out[:16].astype(F32), 16)
    pl.when(early)(lambda: spread(xs.at[0], 0, raw_out[...].astype(F32), rows))
    for g in range(3):
        kept[pl.ds(g * HEAD * SUB, HEAD * SUB), :] = xs[g, : HEAD * SUB, :]
    decay, weight, direct = constants(kept)

    def conv_step(step, early):
        at = step * GROUP
        kv = products(*(short_conv(xs.at[g], kept, g, at + HEAD) for g in (1, 2)))
        for i in range(GROUP):
            base_out[at + i] = kv[i]
        if early:
            for i, value in enumerate(short_conv(xs.at[0], kept, 0, at + HEAD)):
                query_out[at + i] = value

    def finish(early):
        def conv(step, carried):
            conv_step(step, early)
            return carried

        def step_fn(step, state):
            if early:
                return scan(step * 4, 4, decay, weight, direct, state, base_out, base_out)
            return advance(step * 4, 4, decay, state, base_out)

        lax.fori_loop(0, (rows - HEAD) // GROUP, conv, 0)
        state = lax.fori_loop(0, (rows - HEAD) // 4, step_fn, nothing())
        for n in range(MODES):
            state_s[n] = state[n]

    pl.when(early)(lambda: finish(True))
    pl.when(jnp.logical_not(early))(lambda: finish(False))

    for n in range(SUB):
        for h, value in enumerate(paired(state_s[n], state_s[n + SUB])):
            rows_s[pl.ds(h * SENT + n, SUB, stride=2 * SENT), :] = value
    for j in range(SUB):
        cols = slice(j * LANES, (j + 1) * LANES)
        ends = [x[rows - 16 :, cols].astype(F32)[16 - HEAD :] for x in projections]
        starts = [x[:16, cols].astype(F32)[:HEAD] for x in projections]
        for at, (first, second) in (
            (FIRST, (starts[1], starts[2])),
            (LAST, (ends[1], ends[2])),
            (LAST + HEAD, (ends[0], ends[0])),
        ):
            for h, value in enumerate(paired(first, second)):
                rows_s[pl.ds((2 * j + h) * SENT + at, HEAD), :] = value
    for d in range(OWNERS):
        message_out[d] = rows_s[pl.ds(d * SENT, SENT), :].astype(BF16)


def owned(source, rows, row_s):
    spot = lax.rem(lax.axis_index("ctx"), OWNERS)
    lanes = pl.ds(pl.multiple_of(lax.div(spot, 2) * LANES, LANES), LANES)
    first, second = source(lanes)
    row_s[0, :rows] = first
    row_s[1, :rows] = second
    lower, upper = paired(row_s[0], row_s[1])
    return jnp.where(lax.rem(spot, 2) == 0, lower, upper)


def own_rates(rates, row_s):
    return owned(lambda lanes: (rates[:SUB, lanes], rates[SUB:, lanes]), SUB, row_s)


def own_taps(taps, row_s):
    return owned(lambda lanes: (taps[1, :, lanes], taps[2, :, lanes]), TAPS, row_s)


def edge_state(before, first, taps, fades):
    window = jnp.concatenate([before, first], 0)
    conv = taps[0:1] * first
    for j in range(1, TAPS):
        conv = conv + taps[j : j + 1] * window[HEAD - j : 2 * HEAD - j]
    product = (conv * swap(conv)).astype(BF16).astype(F32)
    total = fades[0] * product[0:1]
    for s in range(1, HEAD):
        total = total + fades[s] * product[s : s + 1]
    return total


def edge_fades(rate, block, length):
    return [jnp.exp(rate * (-float(block - 1 - s) / length)) for s in range(HEAD)]


def meet_kernel(block, length, teams, met, rates, taps, states_out, sent_out, row_s):
    rate = own_rates(rates, row_s)
    weights = own_taps(taps, row_s)
    fades = edge_fades(rate, block, length)
    step = jnp.exp(rate * (-float(block) / length))
    total = None
    before = None
    for d in range(OWNERS):
        rows = met[d].astype(F32)
        state = rows[:SUB]
        if d:
            state = state + edge_state(before, rows[FIRST : FIRST + HEAD], weights, fades)
        states_out[d] = state
        total = state if d == 0 else step * total + state
        before = rows[LAST : LAST + HEAD]
    ending = met[OWNERS - 1].astype(F32)[LAST:].astype(BF16)
    opening = met[0].astype(F32)[FIRST : FIRST + HEAD]
    beginning = jnp.concatenate([total, opening], 0).astype(BF16)
    for m in range(teams):
        sent_out[m, :16] = ending
        sent_out[m, 16:] = beginning


def carry_kernel(block, length, teams, gathered, states, met, rates, taps, back_out, row_s, edge_s):
    mine = lax.div(lax.axis_index("ctx"), OWNERS)
    rate = own_rates(rates, row_s)
    weights = own_taps(taps, row_s)
    fades = edge_fades(rate, block, length)
    whole_team = float(block * OWNERS) / length
    to_end = jnp.exp(rate * (-float(block * (OWNERS - 1)) / length))
    carry = jnp.zeros((SUB, LANES), F32)
    before = jnp.zeros((HEAD, LANES), F32)
    edge_s[0, :HEAD] = before
    edge_s[0, HEAD : 2 * HEAD] = before
    for m in range(teams):
        rows = gathered[m].astype(F32)
        edge = edge_state(before, rows[24:], weights, fades)
        edge_s[m, 2 * HEAD :] = edge
        gap = jnp.maximum(mine - 1 - m, 0).astype(F32) * whole_team
        share = jnp.exp(-(rate * gap)) * (rows[16:24] + to_end * edge)
        carry = carry + jnp.where(m < mine, share, 0.0)
        before = rows[:HEAD]
        if m + 1 < teams:
            edge_s[m + 1, : 2 * HEAD] = rows[: 2 * HEAD]
    step = jnp.exp(rate * (-float(block) / length))
    here = edge_s[mine]
    for d in range(OWNERS):
        if d == 0:
            ahead = here[: 2 * HEAD]
        else:
            ahead = met[d - 1].astype(F32)[LAST:]
        back_out[d] = jnp.concatenate([carry, ahead], 0).astype(BF16)
        state = states[d]
        if d == 0:
            state = state + here[2 * HEAD :]
        carry = step * carry + state


def gate_kernel(
    back,
    kept,
    base,
    query,
    raw,
    gated_out,
    squares_out,
    xs,
    base_head,
    query_head,
    rows_s,
    tiles,
    raw_s,
    base_s,
    query_s,
):
    rest = base.shape[0]
    rows = HEAD + rest
    for g in range(3):
        xs[g, HEAD * SUB :] = kept[pl.ds(g * HEAD * SUB, HEAD * SUB), :]
    for d in range(OWNERS):
        rows_s[pl.ds(d * BACK, BACK), :] = back[d].astype(F32)

    def received(row):
        return paired(
            rows_s[pl.ds(row, SUB, stride=2 * BACK), :],
            rows_s[pl.ds(BACK + row, SUB, stride=2 * BACK), :],
        )

    for r in range(HEAD):
        key, value = received(SUB + r)
        xs[1, r * SUB : (r + 1) * SUB] = key
        xs[2, r * SUB : (r + 1) * SUB] = value
        xs[0, r * SUB : (r + 1) * SUB] = received(SUB + HEAD + r)[0]
    kv = products(*(short_conv(xs.at[g], kept, g, HEAD) for g in (1, 2)))
    for i, value in enumerate(short_conv(xs.at[0], kept, 0, HEAD)):
        query_head[i] = value
        base_head[i] = kv[i]
    decay, weight, direct = constants(kept)
    entered = scan(0, HEAD, decay, weight, direct, nothing(), base_head, base_head)
    state = [None] * MODES
    for n in range(SUB):
        for value, m in zip(received(n), (n, n + SUB)):
            state[m] = decay[m] * weight[m] * value

    def four(first, base, query, at, state):
        for i in range(4):
            value = query[first + i] * (base[first + i] + tree_sum(list(state)))
            tiles[pl.ds(pl.multiple_of((at + i) * SUB, SUB), SUB), :] = value
            state = [decay[n] * state[n] for n in range(MODES)]
        return tuple(state)

    for at in range(0, HEAD, 4):
        state = four(at, base_head, query_head, at, state)
    state = tuple(state[n] + decay[n] * weight[n] * entered[n] for n in range(MODES))

    def apply(base, query):
        lax.fori_loop(
            0,
            rest // 4,
            lambda step, held: four(step * 4, base, query, step * 4 + HEAD, held),
            state,
        )

    def own_output():
        spread(raw_s, 0, raw[...].astype(F32), rows)

        def conv(step, carried):
            at = step * GROUP
            for i, value in enumerate(short_conv(raw_s, kept, 0, at + HEAD)):
                query_s[at + i] = value
            return carried

        lax.fori_loop(0, rest // GROUP, conv, 0)
        lax.fori_loop(
            0,
            rest // 4,
            lambda step, held: scan(step * 4, 4, decay, weight, direct, held, base, base_s),
            nothing(),
        )
        apply(base_s, query_s)

    early = is_early()
    pl.when(early)(lambda: apply(base, query))
    pl.when(jnp.logical_not(early))(own_output)
    squares = jnp.zeros((rows, LANES), F32)
    for j in range(SUB):
        part = tiles[pl.ds(j, rows, stride=SUB), :]
        gated_out[:, j * LANES : (j + 1) * LANES] = part
        squares = squares + part * part
    ones = jnp.ones((SUB, LANES), F32)
    line = lax.dot_general(
        ones, squares, (((1,), (1,)), ((), ())), precision=HIGHEST, preferred_element_type=F32
    )
    squares_out[...] = line[: squares_out.shape[0]]


def norm_kernel(width, gated, squares, gain, out):
    count = squares.shape[0]
    ones = jnp.ones((count, LANES), F32)
    total = lax.dot_general(
        squares[...], ones, (((0,), (0,)), ((), ())), precision=HIGHEST, preferred_element_type=F32
    )
    scale = lax.rsqrt(total * (1.0 / width) + 1e-05)
    for j in range(SUB):
        cols = slice(j * LANES, (j + 1) * LANES)
        out[:, cols] = (gated[:, cols] * gain[:, cols] * scale).astype(out.dtype)


def on_chip(mebibytes):
    return pltpu.CompilerParams(vmem_limit_bytes=mebibytes << 20)


def array(*shape):
    return jax.ShapeDtypeStruct(shape, F32)


def shards(projected, short_taps, residues, rates, skip_gain, norm_gain):
    rows = projected.shape[0]
    channels = projected.shape[2]
    groups = lax.axis_size("ctx")
    parts = lax.axis_size("tp")
    teams = groups // OWNERS
    length = rows * groups
    in_team = [[m * OWNERS + d for d in range(OWNERS)] for m in range(teams)]
    across = [[m * OWNERS + d for m in range(teams)] for d in range(OWNERS)]

    proj = jnp.transpose(projected, (1, 0, 2))
    rate_t = rates.T
    residue_t = residues.T
    skip = skip_gain.reshape(SUB, LANES)
    block_tiles = pltpu.VMEM((rows - HEAD, SUB, LANES), F32)
    head_tiles = pltpu.VMEM((HEAD, SUB, LANES), F32)
    row_pair = pltpu.VMEM((2, SUB, LANES), F32)
    inputs = (proj, short_taps, rate_t, residue_t, skip)
    message, base, query, kept, raw = pl.pallas_call(
        lambda *refs: local_kernel(length, *refs),
        name="local",
        out_shape=(
            jax.ShapeDtypeStruct((OWNERS, SENT, LANES), BF16),
            array(rows - HEAD, SUB, LANES),
            array(rows - HEAD, SUB, LANES),
            array(KEPT * SUB, LANES),
            jax.ShapeDtypeStruct((rows, channels), BF16),
        ),
        in_specs=[whole(pltpu.HBM)] * 5,
        out_specs=(whole(),) * 5,
        scratch_shapes=[pltpu.VMEM((2, rows, channels), BF16)]
        + [pltpu.VMEM(x.shape, x.dtype) for x in inputs[1:4]]
        + [
            pltpu.VMEM((3, rows * SUB, LANES), F32),
            pltpu.VMEM((MODES, SUB, LANES), F32),
            pltpu.VMEM((OWNERS * SENT, LANES), F32),
            pltpu.SemaphoreType.DMA((7,)),
        ],
        compiler_params=on_chip(32),
    )(*(pltpu.with_memory_space_constraint(x, pltpu.HBM) for x in inputs))

    met = lax.all_to_all(message, "ctx", 0, 0, tiled=True, axis_index_groups=in_team)
    states, sent = pl.pallas_call(
        lambda *refs: meet_kernel(rows, length, teams, *refs),
        name="meet",
        out_shape=(
            array(OWNERS, SUB, LANES),
            jax.ShapeDtypeStruct((teams, 4 * HEAD, LANES), BF16),
        ),
        in_specs=[whole()] * 3,
        out_specs=(whole(),) * 2,
        scratch_shapes=[row_pair],
        compiler_params=on_chip(4),
    )(met, rate_t, short_taps)
    gathered = lax.all_to_all(sent, "ctx", 0, 0, tiled=True, axis_index_groups=across)
    back = pl.pallas_call(
        lambda *refs: carry_kernel(rows, length, teams, *refs),
        name="carry",
        out_shape=jax.ShapeDtypeStruct((OWNERS, BACK, LANES), BF16),
        in_specs=[whole()] * 5,
        out_specs=whole(),
        scratch_shapes=[row_pair, pltpu.VMEM((teams, 3 * HEAD, LANES), F32)],
        compiler_params=on_chip(4),
    )(gathered, states, met, rate_t, short_taps)
    back = lax.all_to_all(back, "ctx", 0, 0, tiled=True, axis_index_groups=in_team)

    gated, squares = pl.pallas_call(
        gate_kernel,
        name="gate",
        out_shape=(array(rows, channels), array(parts, rows)),
        in_specs=[whole()] * 5,
        out_specs=(whole(),) * 2,
        scratch_shapes=[
            pltpu.VMEM((3, 2 * HEAD * SUB, LANES), F32),
            head_tiles,
            head_tiles,
            pltpu.VMEM((OWNERS * BACK, LANES), F32),
            pltpu.VMEM((rows * SUB, LANES), F32),
            pltpu.VMEM((rows * SUB, LANES), F32),
            block_tiles,
            block_tiles,
        ],
        compiler_params=on_chip(16),
    )(back, kept, base, query, raw)
    squares = lax.all_to_all(squares, "tp", 0, 0, tiled=True)
    return pl.pallas_call(
        lambda *refs: norm_kernel(channels * parts, *refs),
        name="norm",
        out_shape=jax.ShapeDtypeStruct((rows, channels), BF16),
        in_specs=[whole()] * 3,
        out_specs=whole(),
        compiler_params=on_chip(4),
    )(gated, squares, norm_gain.reshape(1, channels))


def solution(mesh):
    return jax.shard_map(
        shards,
        mesh=mesh,
        in_specs=(
            P("ctx", None, "tp"),
            P(None, None, "tp"),
            P("tp", None),
            P("tp", None),
            P("tp"),
            P("tp"),
        ),
        out_specs=P("ctx", "tp"),
        check_vma=False,
    )
```

```python
import math

import jax
import jax.numpy as jnp
from jax import lax
from jax.experimental import pallas as pl
from jax.experimental.pallas import tpu as pltpu
from jax.sharding import PartitionSpec as P

TAPS = 7
MODES = 16
LANES = 128
SUB = 8
OWNERS = 16
HALF = LANES // 2
HEAD = 8
GROUP = 8
FIRST, LAST, SENT = 8, 16, 32
BACK = 24
TAP_AT = 3 * HEAD
DECAY_AT = TAP_AT + 3 * TAPS
WEIGHT_AT = DECAY_AT + MODES
SKIP_AT = WEIGHT_AT + MODES
KEPT = SKIP_AT + 1
EARLY = 2
HIGHEST = lax.Precision.HIGHEST
F32 = jnp.float32
BF16 = jnp.bfloat16


def whole(memory_space=pltpu.VMEM):
    return pl.BlockSpec(memory_space=memory_space)


def spread(dst, base, src, rows):
    for j in range(SUB):
        dst[pl.ds(base * SUB + j, rows, stride=SUB), :] = src[:, j * LANES : (j + 1) * LANES]


def tile(ref, row):
    return ref[pl.ds(pl.multiple_of(row * SUB, SUB), SUB), :]


def tree_sum(parts):
    while len(parts) > 1:
        parts = [parts[k] + parts[k + 1] for k in range(0, len(parts), 2)]
    return parts[0]


def swap(x):
    return pltpu.roll(x, HALF, 1)


def paired(first, second):
    low = lax.broadcasted_iota(jnp.int32, first.shape, 1) < HALF
    return jnp.where(low, first, swap(second)), jnp.where(low, swap(first), second)


def short_conv(xs, kept, g, first):
    window = [tile(xs, first - (TAPS - 1) + i) for i in range(GROUP + TAPS - 1)]
    weights = [tile(kept, TAP_AT + g * TAPS + j) for j in range(TAPS)]
    outs = []
    for i in range(GROUP):
        total = weights[0] * window[i + TAPS - 1]
        for j in range(1, TAPS):
            total = total + weights[j] * window[i + TAPS - 1 - j]
        outs.append(total)
    return outs


def products(keys, values):
    return [(k * v).astype(BF16).astype(F32) for k, v in zip(keys, values)]


def constants(kept):
    decay = [tile(kept, DECAY_AT + n) for n in range(MODES)]
    weight = [tile(kept, WEIGHT_AT + n) for n in range(MODES)]
    return decay, weight, tile(kept, SKIP_AT)


def advance(first, count, decay, state, source):
    state = list(state)
    for i in range(count):
        kv = source[first + i]
        state = [decay[n] * state[n] + kv for n in range(MODES)]
    return tuple(state)


def scan(first, count, decay, weight, direct, state, source, dest):
    state = list(state)
    for i in range(count):
        kv = source[first + i]
        state = [decay[n] * state[n] + kv for n in range(MODES)]
        dest[first + i] = direct * kv + tree_sum([weight[n] * state[n] for n in range(MODES)])
    return tuple(state)


def nothing():
    return (jnp.zeros((SUB, LANES), F32),) * MODES


def is_early():
    return lax.axis_index("ctx") < EARLY * OWNERS


def local_kernel(
    length,
    proj_hbm,
    taps_hbm,
    rates_hbm,
    residues_hbm,
    skip_hbm,
    message_out,
    base_out,
    query_out,
    kept,
    raw_out,
    proj,
    taps,
    rates,
    residues,
    xs,
    state_s,
    rows_s,
    arrived,
):
    pieces = [
        (proj_hbm.at[1], proj.at[0]),
        (proj_hbm.at[2], proj.at[1]),
        (proj_hbm.at[0], raw_out),
    ]
    projections = (raw_out, proj.at[0], proj.at[1])
    pieces[2:2] = [
        (taps_hbm, taps),
        (rates_hbm, rates),
        (residues_hbm, residues),
        (skip_hbm, kept.at[pl.ds(SKIP_AT * SUB, SUB)]),
    ]
    copies = [
        pltpu.make_async_copy(src, dst, arrived.at[i]) for i, (src, dst) in enumerate(pieces)
    ]
    for copy in copies:
        copy.start()
    rows = raw_out.shape[0]
    for g, copy in ((1, copies[0]), (2, copies[1])):
        copy.wait()
        spread(xs.at[g], 0, projections[g][...].astype(F32), rows)
    for copy in copies[2:6]:
        copy.wait()
    for g in range(3):
        spread(kept, TAP_AT + g * TAPS, taps[g], TAPS)
    spread(kept, DECAY_AT, jnp.exp(rates[...] * (-1.0 / length)), MODES)
    spread(kept, WEIGHT_AT, residues[...] * (1.0 / math.sqrt(length)), MODES)
    copies[6].wait()
    early = is_early()
    spread(xs.at[0], 0, raw_out[:16].astype(F32), 16)
    pl.when(early)(lambda: spread(xs.at[0], 0, raw_out[...].astype(F32), rows))
    for g in range(3):
        kept[pl.ds(g * HEAD * SUB, HEAD * SUB), :] = xs[g, : HEAD * SUB, :]
    decay, weight, direct = constants(kept)

    def conv_step(step, early):
        at = step * GROUP
        kv = products(*(short_conv(xs.at[g], kept, g, at + HEAD) for g in (1, 2)))
        for i in range(GROUP):
            base_out[at + i] = kv[i]
        if early:
            for i, value in enumerate(short_conv(xs.at[0], kept, 0, at + HEAD)):
                query_out[at + i] = value

    def finish(early):
        def conv(step, carried):
            conv_step(step, early)
            return carried

        def step_fn(step, state):
            if early:
                return scan(step * 4, 4, decay, weight, direct, state, base_out, base_out)
            return advance(step * 4, 4, decay, state, base_out)

        lax.fori_loop(0, (rows - HEAD) // GROUP, conv, 0)
        state = lax.fori_loop(0, (rows - HEAD) // 4, step_fn, nothing())
        for n in range(MODES):
            state_s[n] = state[n]

    pl.when(early)(lambda: finish(True))
    pl.when(jnp.logical_not(early))(lambda: finish(False))

    for n in range(SUB):
        for h, value in enumerate(paired(state_s[n], state_s[n + SUB])):
            rows_s[pl.ds(h * SENT + n, SUB, stride=2 * SENT), :] = value
    for j in range(SUB):
        cols = slice(j * LANES, (j + 1) * LANES)
        ends = [x[rows - 16 :, cols].astype(F32)[16 - HEAD :] for x in projections]
        starts = [x[:16, cols].astype(F32)[:HEAD] for x in projections]
        for at, (first, second) in (
            (FIRST, (starts[1], starts[2])),
            (LAST, (ends[1], ends[2])),
            (LAST + HEAD, (ends[0], ends[0])),
        ):
            for h, value in enumerate(paired(first, second)):
                rows_s[pl.ds((2 * j + h) * SENT + at, HEAD), :] = value
    for d in range(OWNERS):
        message_out[d] = rows_s[pl.ds(d * SENT, SENT), :].astype(BF16)


def owned(source, rows, row_s):
    spot = lax.rem(lax.axis_index("ctx"), OWNERS)
    lanes = pl.ds(pl.multiple_of(lax.div(spot, 2) * LANES, LANES), LANES)
    first, second = source(lanes)
    row_s[0, :rows] = first
    row_s[1, :rows] = second
    lower, upper = paired(row_s[0], row_s[1])
    return jnp.where(lax.rem(spot, 2) == 0, lower, upper)


def own_rates(rates, row_s):
    return owned(lambda lanes: (rates[:SUB, lanes], rates[SUB:, lanes]), SUB, row_s)


def own_taps(taps, row_s):
    return owned(lambda lanes: (taps[1, :, lanes], taps[2, :, lanes]), TAPS, row_s)


def edge_state(before, first, taps, fades):
    window = jnp.concatenate([before, first], 0)
    conv = taps[0:1] * first
    for j in range(1, TAPS):
        conv = conv + taps[j : j + 1] * window[HEAD - j : 2 * HEAD - j]
    product = (conv * swap(conv)).astype(BF16).astype(F32)
    total = fades[0] * product[0:1]
    for s in range(1, HEAD):
        total = total + fades[s] * product[s : s + 1]
    return total


def edge_fades(rate, block, length):
    return [jnp.exp(rate * (-float(block - 1 - s) / length)) for s in range(HEAD)]


def meet_kernel(block, length, teams, met, rates, taps, states_out, sent_out, row_s):
    rate = own_rates(rates, row_s)
    weights = own_taps(taps, row_s)
    fades = edge_fades(rate, block, length)
    step = jnp.exp(rate * (-float(block) / length))
    total = None
    before = None
    for d in range(OWNERS):
        rows = met[d].astype(F32)
        state = rows[:SUB]
        if d:
            state = state + edge_state(before, rows[FIRST : FIRST + HEAD], weights, fades)
        states_out[d] = state
        total = state if d == 0 else step * total + state
        before = rows[LAST : LAST + HEAD]
    ending = met[OWNERS - 1].astype(F32)[LAST:].astype(BF16)
    opening = met[0].astype(F32)[FIRST : FIRST + HEAD]
    beginning = jnp.concatenate([total, opening], 0).astype(BF16)
    for m in range(teams):
        sent_out[m, :16] = ending
        sent_out[m, 16:] = beginning


def carry_kernel(block, length, teams, gathered, states, met, rates, taps, back_out, row_s, edge_s):
    mine = lax.div(lax.axis_index("ctx"), OWNERS)
    rate = own_rates(rates, row_s)
    weights = own_taps(taps, row_s)
    fades = edge_fades(rate, block, length)
    whole_team = float(block * OWNERS) / length
    to_end = jnp.exp(rate * (-float(block * (OWNERS - 1)) / length))
    carry = jnp.zeros((SUB, LANES), F32)
    before = jnp.zeros((HEAD, LANES), F32)
    edge_s[0, :HEAD] = before
    edge_s[0, HEAD : 2 * HEAD] = before
    for m in range(teams):
        rows = gathered[m].astype(F32)
        edge = edge_state(before, rows[24:], weights, fades)
        edge_s[m, 2 * HEAD :] = edge
        gap = jnp.maximum(mine - 1 - m, 0).astype(F32) * whole_team
        share = jnp.exp(-(rate * gap)) * (rows[16:24] + to_end * edge)
        carry = carry + jnp.where(m < mine, share, 0.0)
        before = rows[:HEAD]
        if m + 1 < teams:
            edge_s[m + 1, : 2 * HEAD] = rows[: 2 * HEAD]
    step = jnp.exp(rate * (-float(block) / length))
    here = edge_s[mine]
    for d in range(OWNERS):
        if d == 0:
            ahead = here[: 2 * HEAD]
        else:
            ahead = met[d - 1].astype(F32)[LAST:]
        back_out[d] = jnp.concatenate([carry, ahead], 0).astype(BF16)
        state = states[d]
        if d == 0:
            state = state + here[2 * HEAD :]
        carry = step * carry + state


def gate_kernel(
    back,
    kept,
    base,
    query,
    raw,
    gated_out,
    squares_out,
    xs,
    base_head,
    query_head,
    rows_s,
    tiles,
    raw_s,
    base_s,
    query_s,
):
    rest = base.shape[0]
    rows = HEAD + rest
    for g in range(3):
        xs[g, HEAD * SUB :] = kept[pl.ds(g * HEAD * SUB, HEAD * SUB), :]
    for d in range(OWNERS):
        rows_s[pl.ds(d * BACK, BACK), :] = back[d].astype(F32)

    def received(row):
        return paired(
            rows_s[pl.ds(row, SUB, stride=2 * BACK), :],
            rows_s[pl.ds(BACK + row, SUB, stride=2 * BACK), :],
        )

    for r in range(HEAD):
        key, value = received(SUB + r)
        xs[1, r * SUB : (r + 1) * SUB] = key
        xs[2, r * SUB : (r + 1) * SUB] = value
        xs[0, r * SUB : (r + 1) * SUB] = received(SUB + HEAD + r)[0]
    kv = products(*(short_conv(xs.at[g], kept, g, HEAD) for g in (1, 2)))
    for i, value in enumerate(short_conv(xs.at[0], kept, 0, HEAD)):
        query_head[i] = value
        base_head[i] = kv[i]
    decay, weight, direct = constants(kept)
    entered = scan(0, HEAD, decay, weight, direct, nothing(), base_head, base_head)
    state = [None] * MODES
    for n in range(SUB):
        for value, m in zip(received(n), (n, n + SUB)):
            state[m] = decay[m] * weight[m] * value

    def four(first, base, query, at, state):
        for i in range(4):
            value = query[first + i] * (base[first + i] + tree_sum(list(state)))
            tiles[pl.ds(pl.multiple_of((at + i) * SUB, SUB), SUB), :] = value
            state = [decay[n] * state[n] for n in range(MODES)]
        return tuple(state)

    for at in range(0, HEAD, 4):
        state = four(at, base_head, query_head, at, state)
    state = tuple(state[n] + decay[n] * weight[n] * entered[n] for n in range(MODES))

    def apply(base, query):
        lax.fori_loop(
            0,
            rest // 4,
            lambda step, held: four(step * 4, base, query, step * 4 + HEAD, held),
            state,
        )

    def own_output():
        spread(raw_s, 0, raw[...].astype(F32), rows)

        def conv(step, carried):
            at = step * GROUP
            for i, value in enumerate(short_conv(raw_s, kept, 0, at + HEAD)):
                query_s[at + i] = value
            return carried

        lax.fori_loop(0, rest // GROUP, conv, 0)
        lax.fori_loop(
            0,
            rest // 4,
            lambda step, held: scan(step * 4, 4, decay, weight, direct, held, base, base_s),
            nothing(),
        )
        apply(base_s, query_s)

    early = is_early()
    pl.when(early)(lambda: apply(base, query))
    pl.when(jnp.logical_not(early))(own_output)
    squares = jnp.zeros((rows, LANES), F32)
    for j in range(SUB):
        part = tiles[pl.ds(j, rows, stride=SUB), :]
        gated_out[:, j * LANES : (j + 1) * LANES] = part
        squares = squares + part * part
    ones = jnp.ones((SUB, LANES), F32)
    line = lax.dot_general(
        ones, squares, (((1,), (1,)), ((), ())), precision=HIGHEST, preferred_element_type=F32
    )
    squares_out[...] = line[: squares_out.shape[0]]


def norm_kernel(width, gated, squares, gain, out):
    count = squares.shape[0]
    ones = jnp.ones((count, LANES), F32)
    total = lax.dot_general(
        squares[...], ones, (((0,), (0,)), ((), ())), precision=HIGHEST, preferred_element_type=F32
    )
    scale = lax.rsqrt(total * (1.0 / width) + 1e-05)
    for j in range(SUB):
        cols = slice(j * LANES, (j + 1) * LANES)
        out[:, cols] = (gated[:, cols] * gain[:, cols] * scale).astype(out.dtype)


def on_chip(mebibytes):
    return pltpu.CompilerParams(vmem_limit_bytes=mebibytes << 20)


def array(*shape):
    return jax.ShapeDtypeStruct(shape, F32)


def shards(projected, short_taps, residues, rates, skip_gain, norm_gain):
    rows = projected.shape[0]
    channels = projected.shape[2]
    groups = lax.axis_size("ctx")
    parts = lax.axis_size("tp")
    teams = groups // OWNERS
    length = rows * groups
    in_team = [[m * OWNERS + d for d in range(OWNERS)] for m in range(teams)]
    across = [[m * OWNERS + d for m in range(teams)] for d in range(OWNERS)]

    proj = jnp.transpose(projected, (1, 0, 2))
    rate_t = rates.T
    residue_t = residues.T
    skip = skip_gain.reshape(SUB, LANES)
    block_tiles = pltpu.VMEM((rows - HEAD, SUB, LANES), F32)
    head_tiles = pltpu.VMEM((HEAD, SUB, LANES), F32)
    row_pair = pltpu.VMEM((2, SUB, LANES), F32)
    inputs = (proj, short_taps, rate_t, residue_t, skip)
    message, base, query, kept, raw = pl.pallas_call(
        lambda *refs: local_kernel(length, *refs),
        name="local",
        out_shape=(
            jax.ShapeDtypeStruct((OWNERS, SENT, LANES), BF16),
            array(rows - HEAD, SUB, LANES),
            array(rows - HEAD, SUB, LANES),
            array(KEPT * SUB, LANES),
            jax.ShapeDtypeStruct((rows, channels), BF16),
        ),
        in_specs=[whole(pltpu.HBM)] * 5,
        out_specs=(whole(),) * 5,
        scratch_shapes=[pltpu.VMEM((2, rows, channels), BF16)]
        + [pltpu.VMEM(x.shape, x.dtype) for x in inputs[1:4]]
        + [
            pltpu.VMEM((3, rows * SUB, LANES), F32),
            pltpu.VMEM((MODES, SUB, LANES), F32),
            pltpu.VMEM((OWNERS * SENT, LANES), F32),
            pltpu.SemaphoreType.DMA((7,)),
        ],
        compiler_params=on_chip(32),
    )(*(pltpu.with_memory_space_constraint(x, pltpu.HBM) for x in inputs))

    message, spot = lax.optimization_barrier((message, lax.axis_index("ctx")))
    met = lax.all_to_all(message, "ctx", 0, 0, tiled=True, axis_index_groups=in_team)
    met, spot = lax.optimization_barrier((met, spot))
    states, sent = pl.pallas_call(
        lambda *refs: meet_kernel(rows, length, teams, *refs),
        name="meet",
        out_shape=(
            array(OWNERS, SUB, LANES),
            jax.ShapeDtypeStruct((teams, 4 * HEAD, LANES), BF16),
        ),
        in_specs=[whole()] * 3,
        out_specs=(whole(),) * 2,
        scratch_shapes=[row_pair],
        compiler_params=on_chip(4),
    )(met, rate_t, short_taps)
    def returned(from_teams):
        back = pl.pallas_call(
            lambda *refs: carry_kernel(rows, length, teams, *refs),
            name="carry",
            out_shape=jax.ShapeDtypeStruct((OWNERS, BACK, LANES), BF16),
            in_specs=[whole()] * 5,
            out_specs=whole(),
            scratch_shapes=[row_pair, pltpu.VMEM((teams, 3 * HEAD, LANES), F32)],
            compiler_params=on_chip(4),
        )(from_teams, states, met, rate_t, short_taps)
        return lax.all_to_all(back, "ctx", 0, 0, tiled=True, axis_index_groups=in_team)

    first_team = spot < OWNERS
    sent, ahead = lax.optimization_barrier(
        (
            sent,
            lax.cond(
                first_team,
                lambda: returned(sent),
                lambda: jnp.zeros((OWNERS, BACK, LANES), BF16),
            ),
        )
    )
    gathered = lax.all_to_all(sent, "ctx", 0, 0, tiled=True, axis_index_groups=across)
    back = lax.cond(first_team, lambda: ahead, lambda: returned(gathered))

    gated, squares = pl.pallas_call(
        gate_kernel,
        name="gate",
        out_shape=(array(rows, channels), array(parts, rows)),
        in_specs=[whole()] * 5,
        out_specs=(whole(),) * 2,
        scratch_shapes=[
            pltpu.VMEM((3, 2 * HEAD * SUB, LANES), F32),
            head_tiles,
            head_tiles,
            pltpu.VMEM((OWNERS * BACK, LANES), F32),
            pltpu.VMEM((rows * SUB, LANES), F32),
            pltpu.VMEM((rows * SUB, LANES), F32),
            block_tiles,
            block_tiles,
        ],
        compiler_params=on_chip(16),
    )(back, kept, base, query, raw)
    squares = lax.all_to_all(squares, "tp", 0, 0, tiled=True)
    return pl.pallas_call(
        lambda *refs: norm_kernel(channels * parts, *refs),
        name="norm",
        out_shape=jax.ShapeDtypeStruct((rows, channels), BF16),
        in_specs=[whole()] * 3,
        out_specs=whole(),
        compiler_params=on_chip(4),
    )(gated, squares, norm_gain.reshape(1, channels))


def solution(mesh):
    return jax.shard_map(
        shards,
        mesh=mesh,
        in_specs=(
            P("ctx", None, "tp"),
            P(None, None, "tp"),
            P("tp", None),
            P("tp", None),
            P("tp"),
            P("tp"),
        ),
        out_specs=P("ctx", "tp"),
        check_vma=False,
    )
```

```python
import math

import jax
import jax.numpy as jnp
from jax import lax
from jax.experimental import pallas as pl
from jax.experimental.pallas import tpu as pltpu
from jax.sharding import PartitionSpec as P

TAPS = 7
MODES = 16
LANES = 128
SUB = 8
OWNERS = 16
HALF = LANES // 2
HEAD = 8
GROUP = 8
FIRST, LAST, SENT = 8, 16, 32
BACK = 24
TAP_AT = 3 * HEAD
DECAY_AT = TAP_AT + 3 * TAPS
WEIGHT_AT = DECAY_AT + MODES
SKIP_AT = WEIGHT_AT + MODES
KEPT = SKIP_AT + 1
EARLY = 2
HIGHEST = lax.Precision.HIGHEST
F32 = jnp.float32
BF16 = jnp.bfloat16


def whole(memory_space=pltpu.VMEM):
    return pl.BlockSpec(memory_space=memory_space)


def spread(dst, base, src, rows):
    for j in range(SUB):
        dst[pl.ds(base * SUB + j, rows, stride=SUB), :] = src[:, j * LANES : (j + 1) * LANES]


def tile(ref, row):
    return ref[pl.ds(pl.multiple_of(row * SUB, SUB), SUB), :]


def tree_sum(parts):
    while len(parts) > 1:
        parts = [parts[k] + parts[k + 1] for k in range(0, len(parts), 2)]
    return parts[0]


def swap(x):
    return pltpu.roll(x, HALF, 1)


def paired(first, second):
    low = lax.broadcasted_iota(jnp.int32, first.shape, 1) < HALF
    return jnp.where(low, first, swap(second)), jnp.where(low, swap(first), second)


def short_conv(xs, kept, g, first):
    window = [tile(xs, first - (TAPS - 1) + i) for i in range(GROUP + TAPS - 1)]
    weights = [tile(kept, TAP_AT + g * TAPS + j) for j in range(TAPS)]
    outs = []
    for i in range(GROUP):
        total = weights[0] * window[i + TAPS - 1]
        for j in range(1, TAPS):
            total = total + weights[j] * window[i + TAPS - 1 - j]
        outs.append(total)
    return outs


def products(keys, values):
    return [(k * v).astype(BF16).astype(F32) for k, v in zip(keys, values)]


def constants(kept):
    decay = [tile(kept, DECAY_AT + n) for n in range(MODES)]
    weight = [tile(kept, WEIGHT_AT + n) for n in range(MODES)]
    return decay, weight, tile(kept, SKIP_AT)


def advance(first, count, decay, state, source):
    state = list(state)
    for i in range(count):
        kv = source[first + i]
        state = [decay[n] * state[n] + kv for n in range(MODES)]
    return tuple(state)


def scan(first, count, decay, weight, direct, state, source, dest):
    state = list(state)
    for i in range(count):
        kv = source[first + i]
        state = [decay[n] * state[n] + kv for n in range(MODES)]
        dest[first + i] = direct * kv + tree_sum([weight[n] * state[n] for n in range(MODES)])
    return tuple(state)


def nothing():
    return (jnp.zeros((SUB, LANES), F32),) * MODES


def is_early():
    return lax.axis_index("ctx") < EARLY * OWNERS


def local_kernel(
    length,
    proj_hbm,
    taps_hbm,
    rates_hbm,
    residues_hbm,
    skip_hbm,
    message_out,
    base_out,
    query_out,
    kept,
    raw_out,
    proj,
    taps,
    rates,
    residues,
    xs,
    state_s,
    rows_s,
    arrived,
):
    pieces = [
        (proj_hbm.at[1], proj.at[0]),
        (proj_hbm.at[2], proj.at[1]),
        (proj_hbm.at[0], raw_out),
    ]
    projections = (raw_out, proj.at[0], proj.at[1])
    pieces[2:2] = [
        (taps_hbm, taps),
        (rates_hbm, rates),
        (residues_hbm, residues),
        (skip_hbm, kept.at[pl.ds(SKIP_AT * SUB, SUB)]),
    ]
    copies = [
        pltpu.make_async_copy(src, dst, arrived.at[i]) for i, (src, dst) in enumerate(pieces)
    ]
    for copy in copies:
        copy.start()
    rows = raw_out.shape[0]
    for g, copy in ((1, copies[0]), (2, copies[1])):
        copy.wait()
        spread(xs.at[g], 0, projections[g][...].astype(F32), rows)
    for copy in copies[2:6]:
        copy.wait()
    for g in range(3):
        spread(kept, TAP_AT + g * TAPS, taps[g], TAPS)
    spread(kept, DECAY_AT, jnp.exp(rates[...] * (-1.0 / length)), MODES)
    spread(kept, WEIGHT_AT, residues[...] * (1.0 / math.sqrt(length)), MODES)
    copies[6].wait()
    early = is_early()
    spread(xs.at[0], 0, raw_out[:16].astype(F32), 16)
    pl.when(early)(lambda: spread(xs.at[0], 0, raw_out[...].astype(F32), rows))
    for g in range(3):
        kept[pl.ds(g * HEAD * SUB, HEAD * SUB), :] = xs[g, : HEAD * SUB, :]
    decay, weight, direct = constants(kept)

    def conv_step(step, early):
        at = step * GROUP
        kv = products(*(short_conv(xs.at[g], kept, g, at + HEAD) for g in (1, 2)))
        for i in range(GROUP):
            base_out[at + i] = kv[i]
        if early:
            for i, value in enumerate(short_conv(xs.at[0], kept, 0, at + HEAD)):
                query_out[at + i] = value

    def finish(early):
        def conv(step, carried):
            conv_step(step, early)
            return carried

        def step_fn(step, state):
            if early:
                return scan(step * 4, 4, decay, weight, direct, state, base_out, base_out)
            return advance(step * 4, 4, decay, state, base_out)

        lax.fori_loop(0, (rows - HEAD) // GROUP, conv, 0)
        state = lax.fori_loop(0, (rows - HEAD) // 4, step_fn, nothing())
        for n in range(MODES):
            state_s[n] = state[n]

    pl.when(early)(lambda: finish(True))
    pl.when(jnp.logical_not(early))(lambda: finish(False))

    for n in range(SUB):
        for h, value in enumerate(paired(state_s[n], state_s[n + SUB])):
            rows_s[pl.ds(h * SENT + n, SUB, stride=2 * SENT), :] = value
    for j in range(SUB):
        cols = slice(j * LANES, (j + 1) * LANES)
        ends = [x[rows - 16 :, cols].astype(F32)[16 - HEAD :] for x in projections]
        starts = [x[:16, cols].astype(F32)[:HEAD] for x in projections]
        for at, (first, second) in (
            (FIRST, (starts[1], starts[2])),
            (LAST, (ends[1], ends[2])),
            (LAST + HEAD, (ends[0], ends[0])),
        ):
            for h, value in enumerate(paired(first, second)):
                rows_s[pl.ds((2 * j + h) * SENT + at, HEAD), :] = value
    for d in range(OWNERS):
        message_out[d] = rows_s[pl.ds(d * SENT, SENT), :].astype(BF16)


def owned(source, rows, row_s):
    spot = lax.rem(lax.axis_index("ctx"), OWNERS)
    lanes = pl.ds(pl.multiple_of(lax.div(spot, 2) * LANES, LANES), LANES)
    first, second = source(lanes)
    row_s[0, :rows] = first
    row_s[1, :rows] = second
    lower, upper = paired(row_s[0], row_s[1])
    return jnp.where(lax.rem(spot, 2) == 0, lower, upper)


def own_rates(rates, row_s):
    return owned(lambda lanes: (rates[:SUB, lanes], rates[SUB:, lanes]), SUB, row_s)


def own_taps(taps, row_s):
    return owned(lambda lanes: (taps[1, :, lanes], taps[2, :, lanes]), TAPS, row_s)


def edge_state(before, first, taps, fades):
    window = jnp.concatenate([before, first], 0)
    conv = taps[0:1] * first
    for j in range(1, TAPS):
        conv = conv + taps[j : j + 1] * window[HEAD - j : 2 * HEAD - j]
    product = (conv * swap(conv)).astype(BF16).astype(F32)
    total = fades[0] * product[0:1]
    for s in range(1, HEAD):
        total = total + fades[s] * product[s : s + 1]
    return total


def edge_fades(rate, block, length):
    return [jnp.exp(rate * (-float(block - 1 - s) / length)) for s in range(HEAD)]


def meet_kernel(block, length, teams, met, rates, taps, states_out, sent_out, row_s):
    rate = own_rates(rates, row_s)
    weights = own_taps(taps, row_s)
    fades = edge_fades(rate, block, length)
    step = jnp.exp(rate * (-float(block) / length))
    total = None
    before = None
    for d in range(OWNERS):
        rows = met[d].astype(F32)
        state = rows[:SUB]
        if d:
            state = state + edge_state(before, rows[FIRST : FIRST + HEAD], weights, fades)
        states_out[d] = state
        total = state if d == 0 else step * total + state
        before = rows[LAST : LAST + HEAD]
    ending = met[OWNERS - 1].astype(F32)[LAST:].astype(BF16)
    opening = met[0].astype(F32)[FIRST : FIRST + HEAD]
    beginning = jnp.concatenate([total, opening], 0).astype(BF16)
    for m in range(teams):
        sent_out[m, :16] = ending
        sent_out[m, 16:] = beginning


def carry_kernel(block, length, teams, gathered, states, met, rates, taps, back_out, row_s, edge_s):
    mine = lax.div(lax.axis_index("ctx"), OWNERS)
    rate = own_rates(rates, row_s)
    weights = own_taps(taps, row_s)
    fades = edge_fades(rate, block, length)
    whole_team = float(block * OWNERS) / length
    to_end = jnp.exp(rate * (-float(block * (OWNERS - 1)) / length))
    carry = jnp.zeros((SUB, LANES), F32)
    before = jnp.zeros((HEAD, LANES), F32)
    edge_s[0, :HEAD] = before
    edge_s[0, HEAD : 2 * HEAD] = before
    for m in range(teams):
        rows = gathered[m].astype(F32)
        edge = edge_state(before, rows[24:], weights, fades)
        edge_s[m, 2 * HEAD :] = edge
        gap = jnp.maximum(mine - 1 - m, 0).astype(F32) * whole_team
        share = jnp.exp(-(rate * gap)) * (rows[16:24] + to_end * edge)
        carry = carry + jnp.where(m < mine, share, 0.0)
        before = rows[:HEAD]
        if m + 1 < teams:
            edge_s[m + 1, : 2 * HEAD] = rows[: 2 * HEAD]
    step = jnp.exp(rate * (-float(block) / length))
    here = edge_s[mine]
    for d in range(OWNERS):
        if d == 0:
            ahead = here[: 2 * HEAD]
        else:
            ahead = met[d - 1].astype(F32)[LAST:]
        back_out[d] = jnp.concatenate([carry, ahead], 0).astype(BF16)
        state = states[d]
        if d == 0:
            state = state + here[2 * HEAD :]
        carry = step * carry + state


def gate_kernel(
    back,
    kept,
    base,
    query,
    raw,
    gated_out,
    squares_out,
    xs,
    base_head,
    query_head,
    rows_s,
    tiles,
    raw_s,
    base_s,
    query_s,
):
    rest = base.shape[0]
    rows = HEAD + rest
    for g in range(3):
        xs[g, HEAD * SUB :] = kept[pl.ds(g * HEAD * SUB, HEAD * SUB), :]
    for d in range(OWNERS):
        rows_s[pl.ds(d * BACK, BACK), :] = back[d].astype(F32)

    def received(row):
        return paired(
            rows_s[pl.ds(row, SUB, stride=2 * BACK), :],
            rows_s[pl.ds(BACK + row, SUB, stride=2 * BACK), :],
        )

    for r in range(HEAD):
        key, value = received(SUB + r)
        xs[1, r * SUB : (r + 1) * SUB] = key
        xs[2, r * SUB : (r + 1) * SUB] = value
        xs[0, r * SUB : (r + 1) * SUB] = received(SUB + HEAD + r)[0]
    kv = products(*(short_conv(xs.at[g], kept, g, HEAD) for g in (1, 2)))
    for i, value in enumerate(short_conv(xs.at[0], kept, 0, HEAD)):
        query_head[i] = value
        base_head[i] = kv[i]
    decay, weight, direct = constants(kept)
    entered = scan(0, HEAD, decay, weight, direct, nothing(), base_head, base_head)
    state = [None] * MODES
    for n in range(SUB):
        for value, m in zip(received(n), (n, n + SUB)):
            state[m] = decay[m] * weight[m] * value

    def four(first, base, query, at, state):
        for i in range(4):
            value = query[first + i] * (base[first + i] + tree_sum(list(state)))
            tiles[pl.ds(pl.multiple_of((at + i) * SUB, SUB), SUB), :] = value
            state = [decay[n] * state[n] for n in range(MODES)]
        return tuple(state)

    for at in range(0, HEAD, 4):
        state = four(at, base_head, query_head, at, state)
    state = tuple(state[n] + decay[n] * weight[n] * entered[n] for n in range(MODES))

    def apply(base, query):
        lax.fori_loop(
            0,
            rest // 4,
            lambda step, held: four(step * 4, base, query, step * 4 + HEAD, held),
            state,
        )

    def own_output():
        spread(raw_s, 0, raw[...].astype(F32), rows)

        def conv(step, carried):
            at = step * GROUP
            for i, value in enumerate(short_conv(raw_s, kept, 0, at + HEAD)):
                query_s[at + i] = value
            return carried

        lax.fori_loop(0, rest // GROUP, conv, 0)
        lax.fori_loop(
            0,
            rest // 4,
            lambda step, held: scan(step * 4, 4, decay, weight, direct, held, base, base_s),
            nothing(),
        )
        apply(base_s, query_s)

    early = is_early()
    pl.when(early)(lambda: apply(base, query))
    pl.when(jnp.logical_not(early))(own_output)
    squares = jnp.zeros((rows, LANES), F32)
    for j in range(SUB):
        part = tiles[pl.ds(j, rows, stride=SUB), :]
        gated_out[:, j * LANES : (j + 1) * LANES] = part
        squares = squares + part * part
    ones = jnp.ones((SUB, LANES), F32)
    line = lax.dot_general(
        ones, squares, (((1,), (1,)), ((), ())), precision=HIGHEST, preferred_element_type=F32
    )
    squares_out[...] = line[: squares_out.shape[0]]


def norm_kernel(width, gated, squares, gain, out):
    count = squares.shape[0]
    ones = jnp.ones((count, LANES), F32)
    total = lax.dot_general(
        squares[...], ones, (((0,), (0,)), ((), ())), precision=HIGHEST, preferred_element_type=F32
    )
    scale = lax.rsqrt(total * (1.0 / width) + 1e-05)
    for j in range(SUB):
        cols = slice(j * LANES, (j + 1) * LANES)
        out[:, cols] = (gated[:, cols] * gain[:, cols] * scale).astype(out.dtype)


def on_chip(mebibytes):
    return pltpu.CompilerParams(vmem_limit_bytes=mebibytes << 20)


def array(*shape):
    return jax.ShapeDtypeStruct(shape, F32)


def shards(projected, short_taps, residues, rates, skip_gain, norm_gain):
    rows = projected.shape[0]
    channels = projected.shape[2]
    groups = lax.axis_size("ctx")
    parts = lax.axis_size("tp")
    teams = groups // OWNERS
    length = rows * groups
    in_team = [[m * OWNERS + d for d in range(OWNERS)] for m in range(teams)]
    across = [[m * OWNERS + d for m in range(teams)] for d in range(OWNERS)]

    proj = jnp.transpose(projected, (1, 0, 2))
    rate_t = rates.T
    residue_t = residues.T
    skip = skip_gain.reshape(SUB, LANES)
    block_tiles = pltpu.VMEM((rows - HEAD, SUB, LANES), F32)
    head_tiles = pltpu.VMEM((HEAD, SUB, LANES), F32)
    row_pair = pltpu.VMEM((2, SUB, LANES), F32)
    inputs = (proj, short_taps, rate_t, residue_t, skip)
    message, base, query, kept, raw = pl.pallas_call(
        lambda *refs: local_kernel(length, *refs),
        name="local",
        out_shape=(
            jax.ShapeDtypeStruct((OWNERS, SENT, LANES), BF16),
            array(rows - HEAD, SUB, LANES),
            array(rows - HEAD, SUB, LANES),
            array(KEPT * SUB, LANES),
            jax.ShapeDtypeStruct((rows, channels), BF16),
        ),
        in_specs=[whole(pltpu.HBM)] * 5,
        out_specs=(whole(),) * 5,
        scratch_shapes=[pltpu.VMEM((2, rows, channels), BF16)]
        + [pltpu.VMEM(x.shape, x.dtype) for x in inputs[1:4]]
        + [
            pltpu.VMEM((3, rows * SUB, LANES), F32),
            pltpu.VMEM((MODES, SUB, LANES), F32),
            pltpu.VMEM((OWNERS * SENT, LANES), F32),
            pltpu.SemaphoreType.DMA((7,)),
        ],
        compiler_params=on_chip(32),
    )(*(pltpu.with_memory_space_constraint(x, pltpu.HBM) for x in inputs))

    def exchanged():
        return lax.all_to_all(message, "ctx", 0, 0, tiled=True, axis_index_groups=in_team)

    def combined(met):
        states, sent = pl.pallas_call(
            lambda *refs: meet_kernel(rows, length, teams, *refs),
            name="meet",
            out_shape=(
                array(OWNERS, SUB, LANES),
                jax.ShapeDtypeStruct((teams, 4 * HEAD, LANES), BF16),
            ),
            in_specs=[whole()] * 3,
            out_specs=(whole(),) * 2,
            scratch_shapes=[row_pair],
            compiler_params=on_chip(4),
        )(met, rate_t, short_taps)
        return sent, states, met

    def returned(from_teams, states, met):
        back = pl.pallas_call(
            lambda *refs: carry_kernel(rows, length, teams, *refs),
            name="carry",
            out_shape=jax.ShapeDtypeStruct((OWNERS, BACK, LANES), BF16),
            in_specs=[whole()] * 5,
            out_specs=whole(),
            scratch_shapes=[row_pair, pltpu.VMEM((teams, 3 * HEAD, LANES), F32)],
            compiler_params=on_chip(4),
        )(from_teams, states, met, rate_t, short_taps)
        return lax.all_to_all(back, "ctx", 0, 0, tiled=True, axis_index_groups=in_team)

    def first_round():
        met = exchanged()
        return met, returned(*combined(met))

    def other_round():
        return exchanged(), jnp.zeros((OWNERS, BACK, LANES), BF16)

    first_team = lax.axis_index("ctx") < OWNERS
    met, ahead = lax.cond(first_team, first_round, other_round)
    sent, states, met = combined(met)
    gathered = lax.all_to_all(sent, "ctx", 0, 0, tiled=True, axis_index_groups=across)
    back = lax.cond(first_team, lambda: ahead, lambda: returned(gathered, states, met))

    gated, squares = pl.pallas_call(
        gate_kernel,
        name="gate",
        out_shape=(array(rows, channels), array(parts, rows)),
        in_specs=[whole()] * 5,
        out_specs=(whole(),) * 2,
        scratch_shapes=[
            pltpu.VMEM((3, 2 * HEAD * SUB, LANES), F32),
            head_tiles,
            head_tiles,
            pltpu.VMEM((OWNERS * BACK, LANES), F32),
            pltpu.VMEM((rows * SUB, LANES), F32),
            pltpu.VMEM((rows * SUB, LANES), F32),
            block_tiles,
            block_tiles,
        ],
        compiler_params=on_chip(16),
    )(back, kept, base, query, raw)
    squares = lax.all_to_all(squares, "tp", 0, 0, tiled=True)
    return pl.pallas_call(
        lambda *refs: norm_kernel(channels * parts, *refs),
        name="norm",
        out_shape=jax.ShapeDtypeStruct((rows, channels), BF16),
        in_specs=[whole()] * 3,
        out_specs=whole(),
        compiler_params=on_chip(4),
    )(gated, squares, norm_gain.reshape(1, channels))


def solution(mesh):
    return jax.shard_map(
        shards,
        mesh=mesh,
        in_specs=(
            P("ctx", None, "tp"),
            P(None, None, "tp"),
            P("tp", None),
            P("tp", None),
            P("tp"),
            P("tp"),
        ),
        out_specs=P("ctx", "tp"),
        check_vma=False,
    )
```

```python
import math

import jax
import jax.numpy as jnp
from jax import lax
from jax.experimental import pallas as pl
from jax.experimental.pallas import tpu as pltpu
from jax.sharding import PartitionSpec as P

TAPS = 7
MODES = 16
LANES = 128
SUB = 8
OWNERS = 16
HALF = LANES // 2
HEAD = 8
GROUP = 8
FIRST, LAST, SENT = 8, 16, 32
BACK = 24
TAP_AT = 3 * HEAD
DECAY_AT = TAP_AT + 3 * TAPS
WEIGHT_AT = DECAY_AT + MODES
SKIP_AT = WEIGHT_AT + MODES
KEPT = SKIP_AT + 1
EARLY = 1
HIGHEST = lax.Precision.HIGHEST
F32 = jnp.float32
BF16 = jnp.bfloat16


def whole(memory_space=pltpu.VMEM):
    return pl.BlockSpec(memory_space=memory_space)


def spread(dst, base, src, rows):
    for j in range(SUB):
        dst[pl.ds(base * SUB + j, rows, stride=SUB), :] = src[:, j * LANES : (j + 1) * LANES]


def tile(ref, row):
    return ref[pl.ds(pl.multiple_of(row * SUB, SUB), SUB), :]


def tree_sum(parts):
    while len(parts) > 1:
        parts = [parts[k] + parts[k + 1] for k in range(0, len(parts), 2)]
    return parts[0]


def swap(x):
    return pltpu.roll(x, HALF, 1)


def paired(first, second):
    low = lax.broadcasted_iota(jnp.int32, first.shape, 1) < HALF
    return jnp.where(low, first, swap(second)), jnp.where(low, swap(first), second)


def short_conv(xs, kept, g, first):
    window = [tile(xs, first - (TAPS - 1) + i) for i in range(GROUP + TAPS - 1)]
    weights = [tile(kept, TAP_AT + g * TAPS + j) for j in range(TAPS)]
    outs = []
    for i in range(GROUP):
        total = weights[0] * window[i + TAPS - 1]
        for j in range(1, TAPS):
            total = total + weights[j] * window[i + TAPS - 1 - j]
        outs.append(total)
    return outs


def products(keys, values):
    return [(k * v).astype(BF16).astype(F32) for k, v in zip(keys, values)]


def constants(kept):
    decay = [tile(kept, DECAY_AT + n) for n in range(MODES)]
    weight = [tile(kept, WEIGHT_AT + n) for n in range(MODES)]
    return decay, weight, tile(kept, SKIP_AT)


def advance(first, count, decay, state, source):
    state = list(state)
    for i in range(count):
        kv = source[first + i]
        state = [decay[n] * state[n] + kv for n in range(MODES)]
    return tuple(state)


def scan(first, count, decay, weight, direct, state, source, dest):
    state = list(state)
    for i in range(count):
        kv = source[first + i]
        state = [decay[n] * state[n] + kv for n in range(MODES)]
        dest[first + i] = direct * kv + tree_sum([weight[n] * state[n] for n in range(MODES)])
    return tuple(state)


def nothing():
    return (jnp.zeros((SUB, LANES), F32),) * MODES


def is_early():
    return lax.div(lax.axis_index("ctx"), OWNERS) == EARLY


def local_kernel(
    length,
    proj_hbm,
    taps_hbm,
    rates_hbm,
    residues_hbm,
    skip_hbm,
    message_out,
    base_out,
    query_out,
    kept,
    raw_out,
    proj,
    taps,
    rates,
    residues,
    xs,
    state_s,
    rows_s,
    arrived,
):
    pieces = [
        (proj_hbm.at[1], proj.at[0]),
        (proj_hbm.at[2], proj.at[1]),
        (proj_hbm.at[0], raw_out),
    ]
    projections = (raw_out, proj.at[0], proj.at[1])
    pieces[2:2] = [
        (taps_hbm, taps),
        (rates_hbm, rates),
        (residues_hbm, residues),
        (skip_hbm, kept.at[pl.ds(SKIP_AT * SUB, SUB)]),
    ]
    copies = [
        pltpu.make_async_copy(src, dst, arrived.at[i]) for i, (src, dst) in enumerate(pieces)
    ]
    for copy in copies:
        copy.start()
    rows = raw_out.shape[0]
    for g, copy in ((1, copies[0]), (2, copies[1])):
        copy.wait()
        spread(xs.at[g], 0, projections[g][...].astype(F32), rows)
    for copy in copies[2:6]:
        copy.wait()
    for g in range(3):
        spread(kept, TAP_AT + g * TAPS, taps[g], TAPS)
    spread(kept, DECAY_AT, jnp.exp(rates[...] * (-1.0 / length)), MODES)
    spread(kept, WEIGHT_AT, residues[...] * (1.0 / math.sqrt(length)), MODES)
    copies[6].wait()
    early = is_early()
    spread(xs.at[0], 0, raw_out[:16].astype(F32), 16)
    pl.when(early)(lambda: spread(xs.at[0], 0, raw_out[...].astype(F32), rows))
    for g in range(3):
        kept[pl.ds(g * HEAD * SUB, HEAD * SUB), :] = xs[g, : HEAD * SUB, :]
    decay, weight, direct = constants(kept)

    def conv_step(step, early):
        at = step * GROUP
        kv = products(*(short_conv(xs.at[g], kept, g, at + HEAD) for g in (1, 2)))
        for i in range(GROUP):
            base_out[at + i] = kv[i]
        if early:
            for i, value in enumerate(short_conv(xs.at[0], kept, 0, at + HEAD)):
                query_out[at + i] = value

    def finish(early):
        def conv(step, carried):
            conv_step(step, early)
            return carried

        def step_fn(step, state):
            if early:
                return scan(step * 8, 8, decay, weight, direct, state, base_out, base_out)
            return advance(step * 8, 8, decay, state, base_out)

        lax.fori_loop(0, (rows - HEAD) // GROUP, conv, 0)
        state = lax.fori_loop(0, (rows - HEAD) // 8, step_fn, nothing())
        for n in range(MODES):
            state_s[n] = state[n]

    pl.when(early)(lambda: finish(True))
    pl.when(jnp.logical_not(early))(lambda: finish(False))

    for n in range(SUB):
        for h, value in enumerate(paired(state_s[n], state_s[n + SUB])):
            rows_s[pl.ds(h * SENT + n, SUB, stride=2 * SENT), :] = value
    for j in range(SUB):
        cols = slice(j * LANES, (j + 1) * LANES)
        ends = [x[rows - 16 :, cols].astype(F32)[16 - HEAD :] for x in projections]
        starts = [x[:16, cols].astype(F32)[:HEAD] for x in projections]
        for at, (first, second) in (
            (FIRST, (starts[1], starts[2])),
            (LAST, (ends[1], ends[2])),
            (LAST + HEAD, (ends[0], ends[0])),
        ):
            for h, value in enumerate(paired(first, second)):
                rows_s[pl.ds((2 * j + h) * SENT + at, HEAD), :] = value
    for d in range(OWNERS):
        message_out[d] = rows_s[pl.ds(d * SENT, SENT), :].astype(BF16)


def owned(source, rows, row_s):
    spot = lax.rem(lax.axis_index("ctx"), OWNERS)
    lanes = pl.ds(pl.multiple_of(lax.div(spot, 2) * LANES, LANES), LANES)
    first, second = source(lanes)
    row_s[0, :rows] = first
    row_s[1, :rows] = second
    lower, upper = paired(row_s[0], row_s[1])
    return jnp.where(lax.rem(spot, 2) == 0, lower, upper)


def own_rates(rates, row_s):
    return owned(lambda lanes: (rates[:SUB, lanes], rates[SUB:, lanes]), SUB, row_s)


def own_taps(taps, row_s):
    return owned(lambda lanes: (taps[1, :, lanes], taps[2, :, lanes]), TAPS, row_s)


def edge_state(before, first, taps, fades):
    window = jnp.concatenate([before, first], 0)
    conv = taps[0:1] * first
    for j in range(1, TAPS):
        conv = conv + taps[j : j + 1] * window[HEAD - j : 2 * HEAD - j]
    product = (conv * swap(conv)).astype(BF16).astype(F32)
    total = fades[0] * product[0:1]
    for s in range(1, HEAD):
        total = total + fades[s] * product[s : s + 1]
    return total


def edge_fades(rate, block, length):
    return [jnp.exp(rate * (-float(block - 1 - s) / length)) for s in range(HEAD)]


def meet_kernel(block, length, teams, met, rates, taps, states_out, sent_out, row_s):
    rate = own_rates(rates, row_s)
    weights = own_taps(taps, row_s)
    fades = edge_fades(rate, block, length)
    step = jnp.exp(rate * (-float(block) / length))
    total = None
    before = None
    for d in range(OWNERS):
        rows = met[d].astype(F32)
        state = rows[:SUB]
        if d:
            state = state + edge_state(before, rows[FIRST : FIRST + HEAD], weights, fades)
        states_out[d] = state
        total = state if d == 0 else step * total + state
        before = rows[LAST : LAST + HEAD]
    ending = met[OWNERS - 1].astype(F32)[LAST:].astype(BF16)
    opening = met[0].astype(F32)[FIRST : FIRST + HEAD]
    beginning = jnp.concatenate([total, opening], 0).astype(BF16)
    for m in range(teams):
        sent_out[m, :16] = ending
        sent_out[m, 16:] = beginning


def carry_kernel(block, length, teams, gathered, states, met, rates, taps, back_out, row_s, edge_s):
    mine = lax.div(lax.axis_index("ctx"), OWNERS)
    rate = own_rates(rates, row_s)
    weights = own_taps(taps, row_s)
    fades = edge_fades(rate, block, length)
    whole_team = float(block * OWNERS) / length
    to_end = jnp.exp(rate * (-float(block * (OWNERS - 1)) / length))
    carry = jnp.zeros((SUB, LANES), F32)
    before = jnp.zeros((HEAD, LANES), F32)
    edge_s[0, :HEAD] = before
    edge_s[0, HEAD : 2 * HEAD] = before
    for m in range(teams):
        rows = gathered[m].astype(F32)
        edge = edge_state(before, rows[24:], weights, fades)
        edge_s[m, 2 * HEAD :] = edge
        gap = jnp.maximum(mine - 1 - m, 0).astype(F32) * whole_team
        share = jnp.exp(-(rate * gap)) * (rows[16:24] + to_end * edge)
        carry = carry + jnp.where(m < mine, share, 0.0)
        before = rows[:HEAD]
        if m + 1 < teams:
            edge_s[m + 1, : 2 * HEAD] = rows[: 2 * HEAD]
    step = jnp.exp(rate * (-float(block) / length))
    here = edge_s[mine]
    for d in range(OWNERS):
        if d == 0:
            ahead = here[: 2 * HEAD]
        else:
            ahead = met[d - 1].astype(F32)[LAST:]
        back_out[d] = jnp.concatenate([carry, ahead], 0).astype(BF16)
        state = states[d]
        if d == 0:
            state = state + here[2 * HEAD :]
        carry = step * carry + state


def gate_kernel(
    back,
    kept,
    base,
    query,
    raw,
    gated_out,
    squares_out,
    xs,
    base_head,
    query_head,
    rows_s,
    tiles,
    raw_s,
    base_s,
    query_s,
):
    rest = base.shape[0]
    rows = HEAD + rest
    for g in range(3):
        xs[g, HEAD * SUB :] = kept[pl.ds(g * HEAD * SUB, HEAD * SUB), :]
    for d in range(OWNERS):
        rows_s[pl.ds(d * BACK, BACK), :] = back[d].astype(F32)

    def received(row):
        return paired(
            rows_s[pl.ds(row, SUB, stride=2 * BACK), :],
            rows_s[pl.ds(BACK + row, SUB, stride=2 * BACK), :],
        )

    for r in range(HEAD):
        key, value = received(SUB + r)
        xs[1, r * SUB : (r + 1) * SUB] = key
        xs[2, r * SUB : (r + 1) * SUB] = value
        xs[0, r * SUB : (r + 1) * SUB] = received(SUB + HEAD + r)[0]
    kv = products(*(short_conv(xs.at[g], kept, g, HEAD) for g in (1, 2)))
    for i, value in enumerate(short_conv(xs.at[0], kept, 0, HEAD)):
        query_head[i] = value
        base_head[i] = kv[i]
    decay, weight, direct = constants(kept)
    entered = scan(0, HEAD, decay, weight, direct, nothing(), base_head, base_head)
    state = [None] * MODES
    for n in range(SUB):
        for value, m in zip(received(n), (n, n + SUB)):
            state[m] = decay[m] * weight[m] * value

    def eight(first, base, query, at, state):
        for i in range(8):
            value = query[first + i] * (base[first + i] + tree_sum(list(state)))
            tiles[pl.ds(pl.multiple_of((at + i) * SUB, SUB), SUB), :] = value
            state = [decay[n] * state[n] for n in range(MODES)]
        return tuple(state)

    state = eight(0, base_head, query_head, 0, state)
    state = tuple(state[n] + decay[n] * weight[n] * entered[n] for n in range(MODES))

    def apply(base, query):
        lax.fori_loop(
            0,
            rest // 8,
            lambda step, held: eight(step * 8, base, query, step * 8 + HEAD, held),
            state,
        )

    def own_output():
        spread(raw_s, 0, raw[...].astype(F32), rows)

        def conv(step, carried):
            at = step * GROUP
            for i, value in enumerate(short_conv(raw_s, kept, 0, at + HEAD)):
                query_s[at + i] = value
            return carried

        lax.fori_loop(0, rest // GROUP, conv, 0)
        lax.fori_loop(
            0,
            rest // 4,
            lambda step, held: scan(step * 4, 4, decay, weight, direct, held, base, base_s),
            nothing(),
        )
        apply(base_s, query_s)

    early = is_early()
    pl.when(early)(lambda: apply(base, query))
    pl.when(jnp.logical_not(early))(own_output)
    squares = jnp.zeros((rows, LANES), F32)
    for j in range(SUB):
        part = tiles[pl.ds(j, rows, stride=SUB), :]
        gated_out[:, j * LANES : (j + 1) * LANES] = part
        squares = squares + part * part
    ones = jnp.ones((SUB, LANES), F32)
    line = lax.dot_general(
        ones, squares, (((1,), (1,)), ((), ())), precision=HIGHEST, preferred_element_type=F32
    )
    squares_out[...] = line[: squares_out.shape[0]]


def norm_kernel(width, gated, squares, gain, out):
    count = squares.shape[0]
    ones = jnp.ones((count, LANES), F32)
    total = lax.dot_general(
        squares[...], ones, (((0,), (0,)), ((), ())), precision=HIGHEST, preferred_element_type=F32
    )
    scale = lax.rsqrt(total * (1.0 / width) + 1e-05)
    for j in range(SUB):
        cols = slice(j * LANES, (j + 1) * LANES)
        out[:, cols] = (gated[:, cols] * gain[:, cols] * scale).astype(out.dtype)


def on_chip(mebibytes):
    return pltpu.CompilerParams(vmem_limit_bytes=mebibytes << 20)


def array(*shape):
    return jax.ShapeDtypeStruct(shape, F32)


def shards(projected, short_taps, residues, rates, skip_gain, norm_gain):
    rows = projected.shape[0]
    channels = projected.shape[2]
    groups = lax.axis_size("ctx")
    parts = lax.axis_size("tp")
    teams = groups // OWNERS
    length = rows * groups
    in_team = [[m * OWNERS + d for d in range(OWNERS)] for m in range(teams)]
    across = [[m * OWNERS + d for m in range(teams)] for d in range(OWNERS)]

    proj = jnp.transpose(projected, (1, 0, 2))
    rate_t = rates.T
    residue_t = residues.T
    skip = skip_gain.reshape(SUB, LANES)
    block_tiles = pltpu.VMEM((rows - HEAD, SUB, LANES), F32)
    head_tiles = pltpu.VMEM((HEAD, SUB, LANES), F32)
    row_pair = pltpu.VMEM((2, SUB, LANES), F32)
    inputs = (proj, short_taps, rate_t, residue_t, skip)
    message, base, query, kept, raw = pl.pallas_call(
        lambda *refs: local_kernel(length, *refs),
        name="local",
        out_shape=(
            jax.ShapeDtypeStruct((OWNERS, SENT, LANES), BF16),
            array(rows - HEAD, SUB, LANES),
            array(rows - HEAD, SUB, LANES),
            array(KEPT * SUB, LANES),
            jax.ShapeDtypeStruct((rows, channels), BF16),
        ),
        in_specs=[whole(pltpu.HBM)] * 5,
        out_specs=(whole(),) * 5,
        scratch_shapes=[pltpu.VMEM((2, rows, channels), BF16)]
        + [pltpu.VMEM(x.shape, x.dtype) for x in inputs[1:4]]
        + [
            pltpu.VMEM((3, rows * SUB, LANES), F32),
            pltpu.VMEM((MODES, SUB, LANES), F32),
            pltpu.VMEM((OWNERS * SENT, LANES), F32),
            pltpu.SemaphoreType.DMA((7,)),
        ],
        compiler_params=on_chip(32),
    )(*(pltpu.with_memory_space_constraint(x, pltpu.HBM) for x in inputs))

    def exchanged():
        return lax.all_to_all(message, "ctx", 0, 0, tiled=True, axis_index_groups=in_team)

    def combined(met):
        states, sent = pl.pallas_call(
            lambda *refs: meet_kernel(rows, length, teams, *refs),
            name="meet",
            out_shape=(
                array(OWNERS, SUB, LANES),
                jax.ShapeDtypeStruct((teams, 4 * HEAD, LANES), BF16),
            ),
            in_specs=[whole()] * 3,
            out_specs=(whole(),) * 2,
            scratch_shapes=[row_pair],
            compiler_params=on_chip(4),
        )(met, rate_t, short_taps)
        return sent, states, met

    def returned(from_teams, states, met):
        back = pl.pallas_call(
            lambda *refs: carry_kernel(rows, length, teams, *refs),
            name="carry",
            out_shape=jax.ShapeDtypeStruct((OWNERS, BACK, LANES), BF16),
            in_specs=[whole()] * 5,
            out_specs=whole(),
            scratch_shapes=[row_pair, pltpu.VMEM((teams, 3 * HEAD, LANES), F32)],
            compiler_params=on_chip(4),
        )(from_teams, states, met, rate_t, short_taps)
        return lax.all_to_all(back, "ctx", 0, 0, tiled=True, axis_index_groups=in_team)

    def first_round():
        met = exchanged()
        return met, returned(*combined(met))

    def other_round():
        return exchanged(), jnp.zeros((OWNERS, BACK, LANES), BF16)

    first_team = lax.axis_index("ctx") < OWNERS
    met, ahead = lax.cond(first_team, first_round, other_round)
    sent, states, met = combined(met)
    gathered = lax.all_to_all(sent, "ctx", 0, 0, tiled=True, axis_index_groups=across)
    back = lax.cond(first_team, lambda: ahead, lambda: returned(gathered, states, met))

    gated, squares = pl.pallas_call(
        gate_kernel,
        name="gate",
        out_shape=(array(rows, channels), array(parts, rows)),
        in_specs=[whole()] * 5,
        out_specs=(whole(),) * 2,
        scratch_shapes=[
            pltpu.VMEM((3, 2 * HEAD * SUB, LANES), F32),
            head_tiles,
            head_tiles,
            pltpu.VMEM((OWNERS * BACK, LANES), F32),
            pltpu.VMEM((rows * SUB, LANES), F32),
            pltpu.VMEM((rows * SUB, LANES), F32),
            block_tiles,
            block_tiles,
        ],
        compiler_params=on_chip(16),
    )(back, kept, base, query, raw)
    squares = lax.all_to_all(squares, "tp", 0, 0, tiled=True)
    return pl.pallas_call(
        lambda *refs: norm_kernel(channels * parts, *refs),
        name="norm",
        out_shape=jax.ShapeDtypeStruct((rows, channels), BF16),
        in_specs=[whole()] * 3,
        out_specs=whole(),
        compiler_params=on_chip(4),
    )(gated, squares, norm_gain.reshape(1, channels))


def solution(mesh):
    return jax.shard_map(
        shards,
        mesh=mesh,
        in_specs=(
            P("ctx", None, "tp"),
            P(None, None, "tp"),
            P("tp", None),
            P("tp", None),
            P("tp"),
            P("tp"),
        ),
        out_specs=P("ctx", "tp"),
        check_vma=False,
    )
```

```python
import math

import jax
import jax.numpy as jnp
from jax import lax
from jax.experimental import pallas as pl
from jax.experimental.pallas import tpu as pltpu
from jax.sharding import PartitionSpec as P

TAPS = 7
MODES = 16
LANES = 128
SUB = 8
OWNERS = 16
HALF = LANES // 2
HEAD = 8
GROUP = 8
FIRST, LAST, SENT = 8, 16, 32
BACK = 24
TAP_AT = 3 * HEAD
DECAY_AT = TAP_AT + 3 * TAPS
WEIGHT_AT = DECAY_AT + MODES
SKIP_AT = WEIGHT_AT + MODES
KEPT = SKIP_AT + 1
EARLY = 1
HIGHEST = lax.Precision.HIGHEST
F32 = jnp.float32
BF16 = jnp.bfloat16


def whole(memory_space=pltpu.VMEM):
    return pl.BlockSpec(memory_space=memory_space)


def spread(dst, base, src, rows):
    for j in range(SUB):
        dst[pl.ds(base * SUB + j, rows, stride=SUB), :] = src[:, j * LANES : (j + 1) * LANES]


def tile(ref, row):
    return ref[pl.ds(pl.multiple_of(row * SUB, SUB), SUB), :]


def tree_sum(parts):
    while len(parts) > 1:
        parts = [parts[k] + parts[k + 1] for k in range(0, len(parts), 2)]
    return parts[0]


def swap(x):
    return pltpu.roll(x, HALF, 1)


def paired(first, second):
    low = lax.broadcasted_iota(jnp.int32, first.shape, 1) < HALF
    return jnp.where(low, first, swap(second)), jnp.where(low, swap(first), second)


def short_conv(xs, kept, g, first):
    window = [tile(xs, first - (TAPS - 1) + i) for i in range(GROUP + TAPS - 1)]
    weights = [tile(kept, TAP_AT + g * TAPS + j) for j in range(TAPS)]
    outs = []
    for i in range(GROUP):
        total = weights[0] * window[i + TAPS - 1]
        for j in range(1, TAPS):
            total = total + weights[j] * window[i + TAPS - 1 - j]
        outs.append(total)
    return outs


def products(keys, values):
    return [(k * v).astype(BF16).astype(F32) for k, v in zip(keys, values)]


def constants(kept):
    decay = [tile(kept, DECAY_AT + n) for n in range(MODES)]
    weight = [tile(kept, WEIGHT_AT + n) for n in range(MODES)]
    return decay, weight, tile(kept, SKIP_AT)


def advance(first, count, decay, state, source):
    state = list(state)
    for i in range(count):
        kv = source[first + i]
        state = [decay[n] * state[n] + kv for n in range(MODES)]
    return tuple(state)


def scan(first, count, decay, weight, direct, state, source, dest):
    state = list(state)
    for i in range(count):
        kv = source[first + i]
        state = [decay[n] * state[n] + kv for n in range(MODES)]
        dest[first + i] = direct * kv + tree_sum([weight[n] * state[n] for n in range(MODES)])
    return tuple(state)


def nothing():
    return (jnp.zeros((SUB, LANES), F32),) * MODES


def is_early():
    return lax.div(lax.axis_index("ctx"), OWNERS) == EARLY


def local_kernel(
    length,
    proj_hbm,
    taps_hbm,
    rates_hbm,
    residues_hbm,
    skip_hbm,
    message_out,
    base_out,
    query_out,
    kept,
    raw_out,
    proj,
    taps,
    rates,
    residues,
    xs,
    state_s,
    rows_s,
    arrived,
):
    pieces = [
        (proj_hbm.at[1], proj.at[0]),
        (proj_hbm.at[2], proj.at[1]),
        (proj_hbm.at[0], raw_out),
    ]
    projections = (raw_out, proj.at[0], proj.at[1])
    pieces[2:2] = [
        (taps_hbm, taps),
        (rates_hbm, rates),
        (residues_hbm, residues),
        (skip_hbm, kept.at[pl.ds(SKIP_AT * SUB, SUB)]),
    ]
    copies = [
        pltpu.make_async_copy(src, dst, arrived.at[i]) for i, (src, dst) in enumerate(pieces)
    ]
    for copy in copies:
        copy.start()
    rows = raw_out.shape[0]
    for g, copy in ((1, copies[0]), (2, copies[1])):
        copy.wait()
        spread(xs.at[g], 0, projections[g][...].astype(F32), rows)
    for copy in copies[2:6]:
        copy.wait()
    for g in range(3):
        spread(kept, TAP_AT + g * TAPS, taps[g], TAPS)
    spread(kept, DECAY_AT, jnp.exp(rates[...] * (-1.0 / length)), MODES)
    spread(kept, WEIGHT_AT, residues[...] * (1.0 / math.sqrt(length)), MODES)
    decay, weight, direct = constants(kept)

    def conv_step(step, early):
        at = step * GROUP
        kv = products(*(short_conv(xs.at[g], kept, g, at + HEAD) for g in (1, 2)))
        for i in range(GROUP):
            base_out[at + i] = kv[i]
        if early:
            for i, value in enumerate(short_conv(xs.at[0], kept, 0, at + HEAD)):
                query_out[at + i] = value

    def finish(early):
        def conv(step, carried):
            conv_step(step, early)
            return carried

        def step_fn(step, state):
            if early:
                return scan(step * 8, 8, decay, weight, direct, state, base_out, base_out)
            return advance(step * 8, 8, decay, state, base_out)

        lax.fori_loop(0, (rows - HEAD) // GROUP, conv, 0)
        state = lax.fori_loop(0, (rows - HEAD) // 8, step_fn, nothing())
        for n in range(MODES):
            state_s[n] = state[n]

    early = is_early()

    @pl.when(early)
    def _():
        copies[6].wait()
        spread(xs.at[0], 0, raw_out[...].astype(F32), rows)
        finish(True)

    @pl.when(jnp.logical_not(early))
    def _():
        finish(False)
        copies[6].wait()
        spread(xs.at[0], 0, raw_out[:16].astype(F32), 16)

    for g in range(3):
        kept[pl.ds(g * HEAD * SUB, HEAD * SUB), :] = xs[g, : HEAD * SUB, :]

    for n in range(SUB):
        for h, value in enumerate(paired(state_s[n], state_s[n + SUB])):
            rows_s[pl.ds(h * SENT + n, SUB, stride=2 * SENT), :] = value
    for j in range(SUB):
        cols = slice(j * LANES, (j + 1) * LANES)
        ends = [x[rows - 16 :, cols].astype(F32)[16 - HEAD :] for x in projections]
        starts = [x[:16, cols].astype(F32)[:HEAD] for x in projections]
        for at, (first, second) in (
            (FIRST, (starts[1], starts[2])),
            (LAST, (ends[1], ends[2])),
            (LAST + HEAD, (ends[0], ends[0])),
        ):
            for h, value in enumerate(paired(first, second)):
                rows_s[pl.ds((2 * j + h) * SENT + at, HEAD), :] = value
    for d in range(OWNERS):
        message_out[d] = rows_s[pl.ds(d * SENT, SENT), :].astype(BF16)


def owned(source, rows, row_s):
    spot = lax.rem(lax.axis_index("ctx"), OWNERS)
    lanes = pl.ds(pl.multiple_of(lax.div(spot, 2) * LANES, LANES), LANES)
    first, second = source(lanes)
    row_s[0, :rows] = first
    row_s[1, :rows] = second
    lower, upper = paired(row_s[0], row_s[1])
    return jnp.where(lax.rem(spot, 2) == 0, lower, upper)


def own_rates(rates, row_s):
    return owned(lambda lanes: (rates[:SUB, lanes], rates[SUB:, lanes]), SUB, row_s)


def own_taps(taps, row_s):
    return owned(lambda lanes: (taps[1, :, lanes], taps[2, :, lanes]), TAPS, row_s)


def edge_state(before, first, taps, fades):
    window = jnp.concatenate([before, first], 0)
    conv = taps[0:1] * first
    for j in range(1, TAPS):
        conv = conv + taps[j : j + 1] * window[HEAD - j : 2 * HEAD - j]
    product = (conv * swap(conv)).astype(BF16).astype(F32)
    total = fades[0] * product[0:1]
    for s in range(1, HEAD):
        total = total + fades[s] * product[s : s + 1]
    return total


def edge_fades(rate, block, length):
    return [jnp.exp(rate * (-float(block - 1 - s) / length)) for s in range(HEAD)]


def meet_kernel(block, length, teams, met, rates, taps, states_out, sent_out, row_s):
    rate = own_rates(rates, row_s)
    weights = own_taps(taps, row_s)
    fades = edge_fades(rate, block, length)
    step = jnp.exp(rate * (-float(block) / length))
    total = None
    before = None
    for d in range(OWNERS):
        rows = met[d].astype(F32)
        state = rows[:SUB]
        if d:
            state = state + edge_state(before, rows[FIRST : FIRST + HEAD], weights, fades)
        states_out[d] = state
        total = state if d == 0 else step * total + state
        before = rows[LAST : LAST + HEAD]
    ending = met[OWNERS - 1].astype(F32)[LAST:].astype(BF16)
    opening = met[0].astype(F32)[FIRST : FIRST + HEAD]
    beginning = jnp.concatenate([total, opening], 0).astype(BF16)
    for m in range(teams):
        sent_out[m, :16] = ending
        sent_out[m, 16:] = beginning


def carry_kernel(block, length, teams, gathered, states, met, rates, taps, back_out, row_s, edge_s):
    mine = lax.div(lax.axis_index("ctx"), OWNERS)
    rate = own_rates(rates, row_s)
    weights = own_taps(taps, row_s)
    fades = edge_fades(rate, block, length)
    whole_team = float(block * OWNERS) / length
    to_end = jnp.exp(rate * (-float(block * (OWNERS - 1)) / length))
    carry = jnp.zeros((SUB, LANES), F32)
    before = jnp.zeros((HEAD, LANES), F32)
    edge_s[0, :HEAD] = before
    edge_s[0, HEAD : 2 * HEAD] = before
    for m in range(teams):
        rows = gathered[m].astype(F32)
        edge = edge_state(before, rows[24:], weights, fades)
        edge_s[m, 2 * HEAD :] = edge
        gap = jnp.maximum(mine - 1 - m, 0).astype(F32) * whole_team
        share = jnp.exp(-(rate * gap)) * (rows[16:24] + to_end * edge)
        carry = carry + jnp.where(m < mine, share, 0.0)
        before = rows[:HEAD]
        if m + 1 < teams:
            edge_s[m + 1, : 2 * HEAD] = rows[: 2 * HEAD]
    step = jnp.exp(rate * (-float(block) / length))
    here = edge_s[mine]
    for d in range(OWNERS):
        if d == 0:
            ahead = here[: 2 * HEAD]
        else:
            ahead = met[d - 1].astype(F32)[LAST:]
        back_out[d] = jnp.concatenate([carry, ahead], 0).astype(BF16)
        state = states[d]
        if d == 0:
            state = state + here[2 * HEAD :]
        carry = step * carry + state


def gate_kernel(
    back,
    kept,
    base,
    query,
    raw,
    gated_out,
    squares_out,
    xs,
    base_head,
    query_head,
    rows_s,
    tiles,
    raw_s,
    base_s,
    query_s,
):
    rest = base.shape[0]
    rows = HEAD + rest
    for g in range(3):
        xs[g, HEAD * SUB :] = kept[pl.ds(g * HEAD * SUB, HEAD * SUB), :]
    for d in range(OWNERS):
        rows_s[pl.ds(d * BACK, BACK), :] = back[d].astype(F32)

    def received(row):
        return paired(
            rows_s[pl.ds(row, SUB, stride=2 * BACK), :],
            rows_s[pl.ds(BACK + row, SUB, stride=2 * BACK), :],
        )

    for r in range(HEAD):
        key, value = received(SUB + r)
        xs[1, r * SUB : (r + 1) * SUB] = key
        xs[2, r * SUB : (r + 1) * SUB] = value
        xs[0, r * SUB : (r + 1) * SUB] = received(SUB + HEAD + r)[0]
    kv = products(*(short_conv(xs.at[g], kept, g, HEAD) for g in (1, 2)))
    for i, value in enumerate(short_conv(xs.at[0], kept, 0, HEAD)):
        query_head[i] = value
        base_head[i] = kv[i]
    decay, weight, direct = constants(kept)
    entered = scan(0, HEAD, decay, weight, direct, nothing(), base_head, base_head)
    state = [None] * MODES
    for n in range(SUB):
        for value, m in zip(received(n), (n, n + SUB)):
            state[m] = decay[m] * weight[m] * value

    def eight(first, base, query, at, state):
        for i in range(8):
            value = query[first + i] * (base[first + i] + tree_sum(list(state)))
            tiles[pl.ds(pl.multiple_of((at + i) * SUB, SUB), SUB), :] = value
            state = [decay[n] * state[n] for n in range(MODES)]
        return tuple(state)

    state = eight(0, base_head, query_head, 0, state)
    state = tuple(state[n] + decay[n] * weight[n] * entered[n] for n in range(MODES))

    def apply(base, query):
        lax.fori_loop(
            0,
            rest // 8,
            lambda step, held: eight(step * 8, base, query, step * 8 + HEAD, held),
            state,
        )

    def own_output():
        spread(raw_s, 0, raw[...].astype(F32), rows)

        def conv(step, carried):
            at = step * GROUP
            for i, value in enumerate(short_conv(raw_s, kept, 0, at + HEAD)):
                query_s[at + i] = value
            return carried

        lax.fori_loop(0, rest // GROUP, conv, 0)
        lax.fori_loop(
            0,
            rest // 4,
            lambda step, held: scan(step * 4, 4, decay, weight, direct, held, base, base_s),
            nothing(),
        )
        apply(base_s, query_s)

    early = is_early()
    pl.when(early)(lambda: apply(base, query))
    pl.when(jnp.logical_not(early))(own_output)
    squares = jnp.zeros((rows, LANES), F32)
    for j in range(SUB):
        part = tiles[pl.ds(j, rows, stride=SUB), :]
        gated_out[:, j * LANES : (j + 1) * LANES] = part
        squares = squares + part * part
    ones = jnp.ones((SUB, LANES), F32)
    line = lax.dot_general(
        ones, squares, (((1,), (1,)), ((), ())), precision=HIGHEST, preferred_element_type=F32
    )
    squares_out[...] = line[: squares_out.shape[0]]


def norm_kernel(width, gated, squares, gain, out):
    count = squares.shape[0]
    ones = jnp.ones((count, LANES), F32)
    total = lax.dot_general(
        squares[...], ones, (((0,), (0,)), ((), ())), precision=HIGHEST, preferred_element_type=F32
    )
    scale = lax.rsqrt(total * (1.0 / width) + 1e-05)
    for j in range(SUB):
        cols = slice(j * LANES, (j + 1) * LANES)
        out[:, cols] = (gated[:, cols] * gain[:, cols] * scale).astype(out.dtype)


def on_chip(mebibytes):
    return pltpu.CompilerParams(vmem_limit_bytes=mebibytes << 20)


def array(*shape):
    return jax.ShapeDtypeStruct(shape, F32)


def shards(projected, short_taps, residues, rates, skip_gain, norm_gain):
    rows = projected.shape[0]
    channels = projected.shape[2]
    groups = lax.axis_size("ctx")
    parts = lax.axis_size("tp")
    teams = groups // OWNERS
    length = rows * groups
    in_team = [[m * OWNERS + d for d in range(OWNERS)] for m in range(teams)]
    across = [[m * OWNERS + d for m in range(teams)] for d in range(OWNERS)]

    proj = jnp.transpose(projected, (1, 0, 2))
    rate_t = rates.T
    residue_t = residues.T
    skip = skip_gain.reshape(SUB, LANES)
    block_tiles = pltpu.VMEM((rows - HEAD, SUB, LANES), F32)
    head_tiles = pltpu.VMEM((HEAD, SUB, LANES), F32)
    row_pair = pltpu.VMEM((2, SUB, LANES), F32)
    inputs = (proj, short_taps, rate_t, residue_t, skip)
    message, base, query, kept, raw = pl.pallas_call(
        lambda *refs: local_kernel(length, *refs),
        name="local",
        out_shape=(
            jax.ShapeDtypeStruct((OWNERS, SENT, LANES), BF16),
            array(rows - HEAD, SUB, LANES),
            array(rows - HEAD, SUB, LANES),
            array(KEPT * SUB, LANES),
            jax.ShapeDtypeStruct((rows, channels), BF16),
        ),
        in_specs=[whole(pltpu.HBM)] * 5,
        out_specs=(whole(),) * 5,
        scratch_shapes=[pltpu.VMEM((2, rows, channels), BF16)]
        + [pltpu.VMEM(x.shape, x.dtype) for x in inputs[1:4]]
        + [
            pltpu.VMEM((3, rows * SUB, LANES), F32),
            pltpu.VMEM((MODES, SUB, LANES), F32),
            pltpu.VMEM((OWNERS * SENT, LANES), F32),
            pltpu.SemaphoreType.DMA((7,)),
        ],
        compiler_params=on_chip(32),
    )(*(pltpu.with_memory_space_constraint(x, pltpu.HBM) for x in inputs))

    def exchanged():
        return lax.all_to_all(message, "ctx", 0, 0, tiled=True, axis_index_groups=in_team)

    def combined(met):
        states, sent = pl.pallas_call(
            lambda *refs: meet_kernel(rows, length, teams, *refs),
            name="meet",
            out_shape=(
                array(OWNERS, SUB, LANES),
                jax.ShapeDtypeStruct((teams, 4 * HEAD, LANES), BF16),
            ),
            in_specs=[whole()] * 3,
            out_specs=(whole(),) * 2,
            scratch_shapes=[row_pair],
            compiler_params=on_chip(4),
        )(met, rate_t, short_taps)
        return sent, states, met

    def returned(from_teams, states, met):
        back = pl.pallas_call(
            lambda *refs: carry_kernel(rows, length, teams, *refs),
            name="carry",
            out_shape=jax.ShapeDtypeStruct((OWNERS, BACK, LANES), BF16),
            in_specs=[whole()] * 5,
            out_specs=whole(),
            scratch_shapes=[row_pair, pltpu.VMEM((teams, 3 * HEAD, LANES), F32)],
            compiler_params=on_chip(4),
        )(from_teams, states, met, rate_t, short_taps)
        return lax.all_to_all(back, "ctx", 0, 0, tiled=True, axis_index_groups=in_team)

    def first_round():
        met = exchanged()
        return met, returned(*combined(met))

    def other_round():
        return exchanged(), jnp.zeros((OWNERS, BACK, LANES), BF16)

    first_team = lax.axis_index("ctx") < OWNERS
    met, ahead = lax.cond(first_team, first_round, other_round)
    sent, states, met = combined(met)
    gathered = lax.all_to_all(sent, "ctx", 0, 0, tiled=True, axis_index_groups=across)
    back = lax.cond(first_team, lambda: ahead, lambda: returned(gathered, states, met))

    gated, squares = pl.pallas_call(
        gate_kernel,
        name="gate",
        out_shape=(array(rows, channels), array(parts, rows)),
        in_specs=[whole()] * 5,
        out_specs=(whole(),) * 2,
        scratch_shapes=[
            pltpu.VMEM((3, 2 * HEAD * SUB, LANES), F32),
            head_tiles,
            head_tiles,
            pltpu.VMEM((OWNERS * BACK, LANES), F32),
            pltpu.VMEM((rows * SUB, LANES), F32),
            pltpu.VMEM((rows * SUB, LANES), F32),
            block_tiles,
            block_tiles,
        ],
        compiler_params=on_chip(16),
    )(back, kept, base, query, raw)
    squares = lax.all_to_all(squares, "tp", 0, 0, tiled=True)
    return pl.pallas_call(
        lambda *refs: norm_kernel(channels * parts, *refs),
        name="norm",
        out_shape=jax.ShapeDtypeStruct((rows, channels), BF16),
        in_specs=[whole()] * 3,
        out_specs=whole(),
        compiler_params=on_chip(4),
    )(gated, squares, norm_gain.reshape(1, channels))


def solution(mesh):
    return jax.shard_map(
        shards,
        mesh=mesh,
        in_specs=(
            P("ctx", None, "tp"),
            P(None, None, "tp"),
            P("tp", None),
            P("tp", None),
            P("tp"),
            P("tp"),
        ),
        out_specs=P("ctx", "tp"),
        check_vma=False,
    )
```

```python
import math

import jax
import jax.numpy as jnp
from jax import lax
from jax.experimental import pallas as pl
from jax.experimental.pallas import tpu as pltpu
from jax.sharding import PartitionSpec as P

TAPS = 7
MODES = 16
LANES = 128
SUB = 8
OWNERS = 16
HALF = LANES // 2
HEAD = 8
GROUP = 8
FIRST, LAST, SENT = 8, 16, 32
BACK = 24
TAP_AT = 3 * HEAD
DECAY_AT = TAP_AT + 3 * TAPS
WEIGHT_AT = DECAY_AT + MODES
SKIP_AT = WEIGHT_AT + MODES
KEPT = SKIP_AT + 1
EARLY = 1
HIGHEST = lax.Precision.HIGHEST
F32 = jnp.float32
BF16 = jnp.bfloat16


def whole(memory_space=pltpu.VMEM):
    return pl.BlockSpec(memory_space=memory_space)


def spread(dst, base, src, rows):
    for j in range(SUB):
        dst[pl.ds(base * SUB + j, rows, stride=SUB), :] = src[:, j * LANES : (j + 1) * LANES]


def tile(ref, row):
    return ref[pl.ds(pl.multiple_of(row * SUB, SUB), SUB), :]


def tree_sum(parts):
    while len(parts) > 1:
        parts = [parts[k] + parts[k + 1] for k in range(0, len(parts), 2)]
    return parts[0]


def swap(x):
    return pltpu.roll(x, HALF, 1)


def paired(first, second):
    low = lax.broadcasted_iota(jnp.int32, first.shape, 1) < HALF
    return jnp.where(low, first, swap(second)), jnp.where(low, swap(first), second)


def short_conv(xs, kept, g, first):
    window = [tile(xs, first - (TAPS - 1) + i) for i in range(GROUP + TAPS - 1)]
    weights = [tile(kept, TAP_AT + g * TAPS + j) for j in range(TAPS)]
    outs = []
    for i in range(GROUP):
        total = weights[0] * window[i + TAPS - 1]
        for j in range(1, TAPS):
            total = total + weights[j] * window[i + TAPS - 1 - j]
        outs.append(total)
    return outs


def products(keys, values):
    return [(k * v).astype(BF16).astype(F32) for k, v in zip(keys, values)]


def constants(kept):
    decay = [tile(kept, DECAY_AT + n) for n in range(MODES)]
    weight = [tile(kept, WEIGHT_AT + n) for n in range(MODES)]
    return decay, weight, tile(kept, SKIP_AT)


def advance(first, count, decay, state, source):
    state = list(state)
    for i in range(count):
        kv = source[first + i]
        state = [decay[n] * state[n] + kv for n in range(MODES)]
    return tuple(state)


def scan(first, count, decay, weight, direct, state, source, dest):
    state = list(state)
    for i in range(count):
        kv = source[first + i]
        state = [decay[n] * state[n] + kv for n in range(MODES)]
        dest[first + i] = direct * kv + tree_sum([weight[n] * state[n] for n in range(MODES)])
    return tuple(state)


def nothing():
    return (jnp.zeros((SUB, LANES), F32),) * MODES


def is_early():
    return lax.div(lax.axis_index("ctx"), OWNERS) == EARLY


def local_kernel(
    length,
    proj_hbm,
    taps_hbm,
    rates_hbm,
    residues_hbm,
    skip_hbm,
    message_out,
    base_out,
    query_out,
    kept,
    raw_out,
    proj,
    taps,
    rates,
    residues,
    xs,
    state_s,
    rows_s,
    arrived,
):
    pieces = [
        (proj_hbm.at[1], proj.at[0]),
        (proj_hbm.at[2], proj.at[1]),
        (proj_hbm.at[0], raw_out),
    ]
    projections = (raw_out, proj.at[0], proj.at[1])
    pieces[:0] = [
        (taps_hbm, taps),
        (rates_hbm, rates),
        (residues_hbm, residues),
        (skip_hbm, kept.at[pl.ds(SKIP_AT * SUB, SUB)]),
    ]
    copies = [
        pltpu.make_async_copy(src, dst, arrived.at[i]) for i, (src, dst) in enumerate(pieces)
    ]
    for copy in copies:
        copy.start()
    rows = raw_out.shape[0]
    for copy in copies[:4]:
        copy.wait()
    for g in range(3):
        spread(kept, TAP_AT + g * TAPS, taps[g], TAPS)
    spread(kept, DECAY_AT, jnp.exp(rates[...] * (-1.0 / length)), MODES)
    spread(kept, WEIGHT_AT, residues[...] * (1.0 / math.sqrt(length)), MODES)
    for g, copy in ((1, copies[4]), (2, copies[5])):
        copy.wait()
        spread(xs.at[g], 0, projections[g][...].astype(F32), rows)
    copies[6].wait()
    early = is_early()
    spread(xs.at[0], 0, raw_out[:16].astype(F32), 16)
    pl.when(early)(lambda: spread(xs.at[0], 0, raw_out[...].astype(F32), rows))
    for g in range(3):
        kept[pl.ds(g * HEAD * SUB, HEAD * SUB), :] = xs[g, : HEAD * SUB, :]
    decay, weight, direct = constants(kept)

    def conv_step(step, early):
        at = step * GROUP
        kv = products(*(short_conv(xs.at[g], kept, g, at + HEAD) for g in (1, 2)))
        for i in range(GROUP):
            base_out[at + i] = kv[i]
        if early:
            for i, value in enumerate(short_conv(xs.at[0], kept, 0, at + HEAD)):
                query_out[at + i] = value

    def finish(early):
        def conv(step, carried):
            conv_step(step, early)
            return carried

        def step_fn(step, state):
            if early:
                return scan(step * 8, 8, decay, weight, direct, state, base_out, base_out)
            return advance(step * 8, 8, decay, state, base_out)

        lax.fori_loop(0, (rows - HEAD) // GROUP, conv, 0)
        state = lax.fori_loop(0, (rows - HEAD) // 8, step_fn, nothing())
        for n in range(MODES):
            state_s[n] = state[n]

    pl.when(early)(lambda: finish(True))
    pl.when(jnp.logical_not(early))(lambda: finish(False))

    for n in range(SUB):
        for h, value in enumerate(paired(state_s[n], state_s[n + SUB])):
            rows_s[pl.ds(h * SENT + n, SUB, stride=2 * SENT), :] = value
    for j in range(SUB):
        cols = slice(j * LANES, (j + 1) * LANES)
        ends = [x[rows - 16 :, cols].astype(F32)[16 - HEAD :] for x in projections]
        starts = [x[:16, cols].astype(F32)[:HEAD] for x in projections]
        for at, (first, second) in (
            (FIRST, (starts[1], starts[2])),
            (LAST, (ends[1], ends[2])),
            (LAST + HEAD, (ends[0], ends[0])),
        ):
            for h, value in enumerate(paired(first, second)):
                rows_s[pl.ds((2 * j + h) * SENT + at, HEAD), :] = value
    for d in range(OWNERS):
        message_out[d] = rows_s[pl.ds(d * SENT, SENT), :].astype(BF16)


def owned(source, rows, row_s):
    spot = lax.rem(lax.axis_index("ctx"), OWNERS)
    lanes = pl.ds(pl.multiple_of(lax.div(spot, 2) * LANES, LANES), LANES)
    first, second = source(lanes)
    row_s[0, :rows] = first
    row_s[1, :rows] = second
    lower, upper = paired(row_s[0], row_s[1])
    return jnp.where(lax.rem(spot, 2) == 0, lower, upper)


def own_rates(rates, row_s):
    return owned(lambda lanes: (rates[:SUB, lanes], rates[SUB:, lanes]), SUB, row_s)


def own_taps(taps, row_s):
    return owned(lambda lanes: (taps[1, :, lanes], taps[2, :, lanes]), TAPS, row_s)


def edge_state(before, first, taps, fades):
    window = jnp.concatenate([before, first], 0)
    conv = taps[0:1] * first
    for j in range(1, TAPS):
        conv = conv + taps[j : j + 1] * window[HEAD - j : 2 * HEAD - j]
    product = (conv * swap(conv)).astype(BF16).astype(F32)
    total = fades[0] * product[0:1]
    for s in range(1, HEAD):
        total = total + fades[s] * product[s : s + 1]
    return total


def edge_fades(rate, block, length):
    return [jnp.exp(rate * (-float(block - 1 - s) / length)) for s in range(HEAD)]


def meet_kernel(block, length, teams, met, rates, taps, states_out, sent_out, row_s):
    rate = own_rates(rates, row_s)
    weights = own_taps(taps, row_s)
    fades = edge_fades(rate, block, length)
    step = jnp.exp(rate * (-float(block) / length))
    total = None
    before = None
    for d in range(OWNERS):
        rows = met[d].astype(F32)
        state = rows[:SUB]
        if d:
            state = state + edge_state(before, rows[FIRST : FIRST + HEAD], weights, fades)
        states_out[d] = state
        total = state if d == 0 else step * total + state
        before = rows[LAST : LAST + HEAD]
    ending = met[OWNERS - 1].astype(F32)[LAST:].astype(BF16)
    opening = met[0].astype(F32)[FIRST : FIRST + HEAD]
    beginning = jnp.concatenate([total, opening], 0).astype(BF16)
    for m in range(teams):
        sent_out[m, :16] = ending
        sent_out[m, 16:] = beginning


def carry_kernel(block, length, teams, gathered, states, met, rates, taps, back_out, row_s, edge_s):
    mine = lax.div(lax.axis_index("ctx"), OWNERS)
    rate = own_rates(rates, row_s)
    weights = own_taps(taps, row_s)
    fades = edge_fades(rate, block, length)
    whole_team = float(block * OWNERS) / length
    to_end = jnp.exp(rate * (-float(block * (OWNERS - 1)) / length))
    carry = jnp.zeros((SUB, LANES), F32)
    before = jnp.zeros((HEAD, LANES), F32)
    edge_s[0, :HEAD] = before
    edge_s[0, HEAD : 2 * HEAD] = before
    for m in range(teams):
        rows = gathered[m].astype(F32)
        edge = edge_state(before, rows[24:], weights, fades)
        edge_s[m, 2 * HEAD :] = edge
        gap = jnp.maximum(mine - 1 - m, 0).astype(F32) * whole_team
        share = jnp.exp(-(rate * gap)) * (rows[16:24] + to_end * edge)
        carry = carry + jnp.where(m < mine, share, 0.0)
        before = rows[:HEAD]
        if m + 1 < teams:
            edge_s[m + 1, : 2 * HEAD] = rows[: 2 * HEAD]
    step = jnp.exp(rate * (-float(block) / length))
    here = edge_s[mine]
    for d in range(OWNERS):
        if d == 0:
            ahead = here[: 2 * HEAD]
        else:
            ahead = met[d - 1].astype(F32)[LAST:]
        back_out[d] = jnp.concatenate([carry, ahead], 0).astype(BF16)
        state = states[d]
        if d == 0:
            state = state + here[2 * HEAD :]
        carry = step * carry + state


def gate_kernel(
    back,
    kept,
    base,
    query,
    raw,
    gated_out,
    squares_out,
    xs,
    base_head,
    query_head,
    rows_s,
    tiles,
    raw_s,
    base_s,
    query_s,
):
    rest = base.shape[0]
    rows = HEAD + rest
    for g in range(3):
        xs[g, HEAD * SUB :] = kept[pl.ds(g * HEAD * SUB, HEAD * SUB), :]
    for d in range(OWNERS):
        rows_s[pl.ds(d * BACK, BACK), :] = back[d].astype(F32)

    def received(row):
        return paired(
            rows_s[pl.ds(row, SUB, stride=2 * BACK), :],
            rows_s[pl.ds(BACK + row, SUB, stride=2 * BACK), :],
        )

    for r in range(HEAD):
        key, value = received(SUB + r)
        xs[1, r * SUB : (r + 1) * SUB] = key
        xs[2, r * SUB : (r + 1) * SUB] = value
        xs[0, r * SUB : (r + 1) * SUB] = received(SUB + HEAD + r)[0]
    kv = products(*(short_conv(xs.at[g], kept, g, HEAD) for g in (1, 2)))
    for i, value in enumerate(short_conv(xs.at[0], kept, 0, HEAD)):
        query_head[i] = value
        base_head[i] = kv[i]
    decay, weight, direct = constants(kept)
    entered = scan(0, HEAD, decay, weight, direct, nothing(), base_head, base_head)
    state = [None] * MODES
    for n in range(SUB):
        for value, m in zip(received(n), (n, n + SUB)):
            state[m] = decay[m] * weight[m] * value

    def eight(first, base, query, at, state):
        for i in range(8):
            value = query[first + i] * (base[first + i] + tree_sum(list(state)))
            tiles[pl.ds(pl.multiple_of((at + i) * SUB, SUB), SUB), :] = value
            state = [decay[n] * state[n] for n in range(MODES)]
        return tuple(state)

    state = eight(0, base_head, query_head, 0, state)
    state = tuple(state[n] + decay[n] * weight[n] * entered[n] for n in range(MODES))

    def apply(base, query):
        lax.fori_loop(
            0,
            rest // 8,
            lambda step, held: eight(step * 8, base, query, step * 8 + HEAD, held),
            state,
        )

    def own_output():
        spread(raw_s, 0, raw[...].astype(F32), rows)

        def conv(step, carried):
            at = step * GROUP
            for i, value in enumerate(short_conv(raw_s, kept, 0, at + HEAD)):
                query_s[at + i] = value
            return carried

        lax.fori_loop(0, rest // GROUP, conv, 0)
        lax.fori_loop(
            0,
            rest // 4,
            lambda step, held: scan(step * 4, 4, decay, weight, direct, held, base, base_s),
            nothing(),
        )
        apply(base_s, query_s)

    early = is_early()
    pl.when(early)(lambda: apply(base, query))
    pl.when(jnp.logical_not(early))(own_output)
    squares = jnp.zeros((rows, LANES), F32)
    for j in range(SUB):
        part = tiles[pl.ds(j, rows, stride=SUB), :]
        gated_out[:, j * LANES : (j + 1) * LANES] = part
        squares = squares + part * part
    ones = jnp.ones((SUB, LANES), F32)
    line = lax.dot_general(
        ones, squares, (((1,), (1,)), ((), ())), precision=HIGHEST, preferred_element_type=F32
    )
    squares_out[...] = line[: squares_out.shape[0]]


def norm_kernel(width, gated, squares, gain, out):
    count = squares.shape[0]
    ones = jnp.ones((count, LANES), F32)
    total = lax.dot_general(
        squares[...], ones, (((0,), (0,)), ((), ())), precision=HIGHEST, preferred_element_type=F32
    )
    scale = lax.rsqrt(total * (1.0 / width) + 1e-05)
    for j in range(SUB):
        cols = slice(j * LANES, (j + 1) * LANES)
        out[:, cols] = (gated[:, cols] * gain[:, cols] * scale).astype(out.dtype)


def on_chip(mebibytes):
    return pltpu.CompilerParams(vmem_limit_bytes=mebibytes << 20)


def array(*shape):
    return jax.ShapeDtypeStruct(shape, F32)


def shards(projected, short_taps, residues, rates, skip_gain, norm_gain):
    rows = projected.shape[0]
    channels = projected.shape[2]
    groups = lax.axis_size("ctx")
    parts = lax.axis_size("tp")
    teams = groups // OWNERS
    length = rows * groups
    in_team = [[m * OWNERS + d for d in range(OWNERS)] for m in range(teams)]
    across = [[m * OWNERS + d for m in range(teams)] for d in range(OWNERS)]

    proj = jnp.transpose(projected, (1, 0, 2))
    rate_t = rates.T
    residue_t = residues.T
    skip = skip_gain.reshape(SUB, LANES)
    block_tiles = pltpu.VMEM((rows - HEAD, SUB, LANES), F32)
    head_tiles = pltpu.VMEM((HEAD, SUB, LANES), F32)
    row_pair = pltpu.VMEM((2, SUB, LANES), F32)
    inputs = (proj, short_taps, rate_t, residue_t, skip)
    message, base, query, kept, raw = pl.pallas_call(
        lambda *refs: local_kernel(length, *refs),
        name="local",
        out_shape=(
            jax.ShapeDtypeStruct((OWNERS, SENT, LANES), BF16),
            array(rows - HEAD, SUB, LANES),
            array(rows - HEAD, SUB, LANES),
            array(KEPT * SUB, LANES),
            jax.ShapeDtypeStruct((rows, channels), BF16),
        ),
        in_specs=[whole(pltpu.HBM)] * 5,
        out_specs=(whole(),) * 5,
        scratch_shapes=[pltpu.VMEM((2, rows, channels), BF16)]
        + [pltpu.VMEM(x.shape, x.dtype) for x in inputs[1:4]]
        + [
            pltpu.VMEM((3, rows * SUB, LANES), F32),
            pltpu.VMEM((MODES, SUB, LANES), F32),
            pltpu.VMEM((OWNERS * SENT, LANES), F32),
            pltpu.SemaphoreType.DMA((7,)),
        ],
        compiler_params=on_chip(32),
    )(*(pltpu.with_memory_space_constraint(x, pltpu.HBM) for x in inputs))

    def exchanged():
        return lax.all_to_all(message, "ctx", 0, 0, tiled=True, axis_index_groups=in_team)

    def combined(met):
        states, sent = pl.pallas_call(
            lambda *refs: meet_kernel(rows, length, teams, *refs),
            name="meet",
            out_shape=(
                array(OWNERS, SUB, LANES),
                jax.ShapeDtypeStruct((teams, 4 * HEAD, LANES), BF16),
            ),
            in_specs=[whole()] * 3,
            out_specs=(whole(),) * 2,
            scratch_shapes=[row_pair],
            compiler_params=on_chip(4),
        )(met, rate_t, short_taps)
        return sent, states, met

    def returned(from_teams, states, met):
        back = pl.pallas_call(
            lambda *refs: carry_kernel(rows, length, teams, *refs),
            name="carry",
            out_shape=jax.ShapeDtypeStruct((OWNERS, BACK, LANES), BF16),
            in_specs=[whole()] * 5,
            out_specs=whole(),
            scratch_shapes=[row_pair, pltpu.VMEM((teams, 3 * HEAD, LANES), F32)],
            compiler_params=on_chip(4),
        )(from_teams, states, met, rate_t, short_taps)
        return lax.all_to_all(back, "ctx", 0, 0, tiled=True, axis_index_groups=in_team)

    def first_round():
        met = exchanged()
        return met, returned(*combined(met))

    def other_round():
        return exchanged(), jnp.zeros((OWNERS, BACK, LANES), BF16)

    first_team = lax.axis_index("ctx") < OWNERS
    met, ahead = lax.cond(first_team, first_round, other_round)
    sent, states, met = combined(met)
    gathered = lax.all_to_all(sent, "ctx", 0, 0, tiled=True, axis_index_groups=across)
    back = lax.cond(first_team, lambda: ahead, lambda: returned(gathered, states, met))

    gated, squares = pl.pallas_call(
        gate_kernel,
        name="gate",
        out_shape=(array(rows, channels), array(parts, rows)),
        in_specs=[whole()] * 5,
        out_specs=(whole(),) * 2,
        scratch_shapes=[
            pltpu.VMEM((3, 2 * HEAD * SUB, LANES), F32),
            head_tiles,
            head_tiles,
            pltpu.VMEM((OWNERS * BACK, LANES), F32),
            pltpu.VMEM((rows * SUB, LANES), F32),
            pltpu.VMEM((rows * SUB, LANES), F32),
            block_tiles,
            block_tiles,
        ],
        compiler_params=on_chip(16),
    )(back, kept, base, query, raw)
    squares = lax.all_to_all(squares, "tp", 0, 0, tiled=True)
    return pl.pallas_call(
        lambda *refs: norm_kernel(channels * parts, *refs),
        name="norm",
        out_shape=jax.ShapeDtypeStruct((rows, channels), BF16),
        in_specs=[whole()] * 3,
        out_specs=whole(),
        compiler_params=on_chip(4),
    )(gated, squares, norm_gain.reshape(1, channels))


def solution(mesh):
    return jax.shard_map(
        shards,
        mesh=mesh,
        in_specs=(
            P("ctx", None, "tp"),
            P(None, None, "tp"),
            P("tp", None),
            P("tp", None),
            P("tp"),
            P("tp"),
        ),
        out_specs=P("ctx", "tp"),
        check_vma=False,
    )
```
